128 devices in a mesh: ctx: 16 (over z, x), head: 8 (over y, core).
Axes of the slice: x: 4, y: 4, z: 4, core: 2. Of those that a mesh axis runs over, the one named last changes fastest.
Arguments:
- queries: bfloat16 [16384, 2048], P(('ctx', 'head')), may hold values from -6 to 6
- keys: bfloat16 [16384, 2048], P(('ctx', 'head')), may hold values from -6 to 6
- values: bfloat16 [16384, 2048], P(('ctx', 'head')), may hold values from -6 to 6
- grads_out: bfloat16 [16384, 2048], P(('ctx', 'head')), may hold values from -6 to 6
- log_decay: float32 [16, 16384], P('head', 'ctx'), may hold values from -0.8 to 0
- ridge: float32 [16], P('head'), may hold values from 0.25 to 2
Outputs:
- grad_queries: bfloat16 [16384, 2048], P(('ctx', 'head'))
- grad_keys: bfloat16 [16384, 2048], P(('ctx', 'head'))
- grad_values: bfloat16 [16384, 2048], P(('ctx', 'head'))
The draws below stay inside these ranges and needn't reach their ends.
All inputs are finite; a program needn't handle non-finite values.
Results may differ from the reference program's by a relative error of at most 0.0085.
Values may be sent and summed in bfloat16 or wider, within the bound.
No kernel may reach another device: no remote copies, remote signals or barrier semaphores. Data moves between devices by JAX's collectives and lax.ppermute only.
A program may use at most 128 MiB of HBM per device.

```python
import math
import jax
import jax.numpy as jnp
from jax import lax

DH = 128
SPAN = 512
SOLVE_STEPS = 8
HEADS = 16
TOKEN_COUNT = 16384


def draw_keys(key, part):
    scale_key = jax.random.fold_in(key, 11)
    base_key = jax.random.fold_in(key, 12)
    columns = jnp.exp(jax.random.uniform(scale_key, (HEADS * DH,), jnp.float32, jnp.log(0.05), jnp.log(1.5)))
    overall = 5.0 / jnp.sqrt(jnp.float32(TOKEN_COUNT))
    base = jnp.clip(jax.random.normal(base_key, (TOKEN_COUNT, HEADS * DH), jnp.float32), -4.0, 4.0)
    return (base * columns[None, :] * overall).astype(jnp.bfloat16)


def draw_log_decay(key, part):
    share = 0.5
    fast = jax.random.uniform(jax.random.fold_in(key, 21), (HEADS, 1), jnp.float32) < share
    base = jnp.where(fast, 1.0 / 40.0, 0.5 / TOKEN_COUNT)
    jitter = jax.random.uniform(jax.random.fold_in(key, 22), (HEADS, TOKEN_COUNT), jnp.float32, 0.5, 1.5)
    region = jnp.exp(jax.random.uniform(jax.random.fold_in(key, 23), (HEADS, 8), jnp.float32, jnp.log(0.5), jnp.log(2.0)))
    spread = jnp.repeat(region, TOKEN_COUNT // 8, axis=1)
    segment_batches = jax.random.randint(jax.random.fold_in(key, 24), (3,), 0, TOKEN_COUNT)
    token_offsets = jnp.arange(TOKEN_COUNT, dtype=jnp.int32)
    masked_out_cells = jnp.any(token_offsets[None, :] == segment_batches[:, None], axis=0)
    drops = jax.random.uniform(jax.random.fold_in(key, 25), (HEADS, TOKEN_COUNT), jnp.float32, 0.22, 0.69)
    rate = base * jitter * spread + jnp.where(masked_out_cells[None, :], drops, 0.0)
    return (-rate).astype(jnp.float32)


def level_of(stream_key, extent, shards, low, largest):
    def one(dim, parts):
        heights = jax.random.uniform(jax.random.fold_in(jax.random.fold_in(stream_key, 6), dim), (parts,), jnp.float32, low / len(shards), largest / len(shards))
        return jnp.repeat(jnp.exp(heights), extent[dim] // parts).reshape((-1,) + (1,) * (len(extent) - dim - 1))

    level = one(*shards[0])
    for cut in shards[1:]:
        level = level * one(*cut)
    return level


def noise(stream_key, extent, scale, limit, pieces=(), kind=jnp.bfloat16):
    array = jax.random.normal(stream_key, extent, jnp.float32) * scale
    if len(pieces) > 0:
        array = level_of(stream_key, extent, pieces, -0.22, 0.18) * array
    return jnp.clip(array, min=-limit, max=limit).astype(kind)


def setup_inputs(seed: int = 0) -> dict:
    key_of = jax.random.split(jax.random.key(seed), 7)
    return {
        "queries": noise(key_of[0], (TOKEN_COUNT, HEADS * DH), 1.0, 6.0, ((0, 128),)),
        "keys": draw_keys(jax.random.fold_in(key_of[6], 71), 0),
        "values": noise(key_of[2], (TOKEN_COUNT, HEADS * DH), 1.0, 6.0, ((0, 128),)),
        "grads_out": noise(key_of[3], (TOKEN_COUNT, HEADS * DH), 1.0, 6.0, ((0, 128),)),
        "log_decay": draw_log_decay(jax.random.fold_in(key_of[6], 71), 0),
        "ridge": jnp.clip(jnp.exp(math.log(2.0) - 2.0794415 * jax.random.uniform(key_of[5], (HEADS,), jnp.float32) ** level_of(key_of[5], (HEADS,), ((0, 8),), -0.2, 0.2)), 0.25, 2.0),
    }


highest = lax.Precision.HIGHEST
epsilon = 1e-06

def product(left, right):
    return jnp.dot(left.astype(jnp.float32), right.astype(jnp.float32), precision=highest, preferred_element_type=jnp.float32)

def mixed(left, right):
    return jnp.dot(left.astype(jnp.bfloat16), right.astype(jnp.bfloat16), preferred_element_type=jnp.float32)

def block_decays(log_gate):
    cumul = jnp.cumsum(log_gate)
    size = log_gate.shape[0]
    rowpos = lax.broadcasted_iota(jnp.int32, (size, size), 0)
    column_position = lax.broadcasted_iota(jnp.int32, (size, size), 1)
    within = jnp.exp(jnp.where(rowpos >= column_position, cumul[:, None] - cumul[None, :], -jnp.inf))
    return (cumul, within)

def multiply_by_matrix(direction, gram, keys, within, start_decay, ridge):
    scores = (within * mixed(direction.astype(jnp.bfloat16), keys.T)).astype(jnp.bfloat16)
    return start_decay[:, None] * product(direction, gram) + mixed(scores, keys) + ridge * direction

def conj_grad(rhs, gram, keys, within, start_decay, ridge):
    solution = jnp.zeros_like(rhs)
    residual = rhs
    direction = rhs
    rho_now = lax.optimization_barrier(jnp.sum(rhs * rhs, axis=-1, keepdims=True))
    for sweep in range(SOLVE_STEPS):
        image = multiply_by_matrix(direction, gram, keys, within, start_decay, ridge)
        step_size = rho_now / (lax.optimization_barrier(jnp.sum(direction * image, axis=-1, keepdims=True)) + epsilon)
        solution = solution + step_size * direction
        residual = residual - step_size * image
        rho_next = lax.optimization_barrier(jnp.sum(residual * residual, axis=-1, keepdims=True))
        direction = residual + rho_next / (rho_now + epsilon) * direction
        rho_now = rho_next
    return solution

def span_solve(gram, value_state, queries, keys, values, grads_out, log_gate, ridge):
    cumul, within = block_decays(log_gate)
    start_decay = jnp.exp(cumul)
    solved = conj_grad(queries.astype(jnp.float32), gram, keys, within, start_decay, ridge)
    scores = (within * mixed(grads_out, values.T)).astype(jnp.bfloat16)
    rhs = start_decay[:, None] * product(grads_out, value_state) + mixed(scores, keys)
    adjoint = conj_grad(rhs, gram, keys, within, start_decay, ridge)
    return (solved, adjoint)

def span_grads(value_memory_state, state_gram, keys, values, grads_out, solved, adjoint, log_gate):
    cumul, within = block_decays(log_gate)
    end_weight = jnp.exp(cumul[-1] - cumul)[:, None]
    solved_low = solved.astype(jnp.bfloat16)
    adjoint_low = adjoint.astype(jnp.bfloat16)
    solved_along_keys = (within * mixed(solved_low, keys.T)).astype(jnp.bfloat16)
    along_adjoint = (within * mixed(adjoint_low, keys.T)).astype(jnp.bfloat16)
    along_values = (within * mixed(grads_out, values.T)).astype(jnp.bfloat16)
    grad_values = mixed(solved_along_keys.T, grads_out) + end_weight * product(keys, value_memory_state.T)
    grad_keys = mixed(along_values.T, solved_low) + end_weight * product(values, value_memory_state)
    grad_keys = grad_keys - mixed(solved_along_keys.T, adjoint_low) - mixed(along_adjoint.T, solved_low)
    grad_keys = grad_keys + end_weight * product(keys, state_gram + state_gram.T)
    return (grad_keys, grad_values)

def one_head(pack):
    queries, keys, values, grads_out, log_gate, ridge = pack
    zeros = jnp.zeros((DH, DH), jnp.float32)

    def forward(carry, items):
        gram, value_state = carry
        qblock, kblock, vblock, gblock, lower_tile = items
        solved, adjoint = span_solve(gram, value_state, qblock, kblock, vblock, gblock, lower_tile, ridge)
        cumul = jnp.cumsum(lower_tile)
        weighted = jnp.exp(cumul[-1] - cumul)[:, None] * kblock.astype(jnp.float32)
        total = jnp.exp(cumul[-1])
        gram_next = total * gram + product(kblock.T, weighted)
        value_next = total * value_state + product(vblock.T, weighted)
        return ((gram_next, value_next), (solved, adjoint))
    init = (zeros, zeros)
    unused, outs = lax.scan(forward, init, (queries, keys, values, grads_out, log_gate))
    solved, adjoint = outs

    def backward(carry, items):
        value_memory_state, state_gram = carry
        kblock, vblock, gblock, sblock, ablock, lower_tile = items
        grad_keys, grad_values = span_grads(value_memory_state, state_gram, kblock, vblock, gblock, sblock, ablock, lower_tile)
        cumul = jnp.cumsum(lower_tile)
        weighted = jnp.exp(cumul)[:, None] * sblock
        total = jnp.exp(cumul[-1])
        value_prev = total * value_memory_state + product(gblock.T, weighted)
        gram_prev = total * state_gram - product(ablock.T, weighted)
        return ((value_prev, gram_prev), (grad_keys, grad_values))
    unused2, grads = lax.scan(backward, init, (keys, values, grads_out, solved, adjoint, log_gate), reverse=True)
    return (adjoint, grads[0], grads[1])

def split_all(block):
    count = TOKEN_COUNT // SPAN
    return block.reshape(count, SPAN, HEADS, DH).transpose(2, 0, 1, 3)

def join_all(block):
    return block.transpose(1, 2, 0, 3).reshape(TOKEN_COUNT, HEADS * DH).astype(jnp.bfloat16)

def reference(queries, keys, values, grads_out, log_decay, ridge):
    count = TOKEN_COUNT // SPAN
    gates = log_decay.reshape(HEADS, count, SPAN)
    pack = (split_all(queries), split_all(keys), split_all(values), split_all(grads_out), gates, ridge)
    adjoint, grad_keys, grad_values = lax.map(one_head, pack)
    return (join_all(adjoint), join_all(grad_keys), join_all(grad_values))
```

```python
import jax
import jax.numpy as jnp
from jax import lax
from jax.experimental import pallas as pl
from jax.experimental.pallas import tpu as pltpu
from jax.sharding import PartitionSpec as P

DH = 128
SPAN = 512
HALF = SPAN // 2
SOLVE_STEPS = 8
EPSILON = 1e-06

F32 = jnp.float32
BF16 = jnp.bfloat16


def dot(left, right):
    return jnp.dot(left, right, preferred_element_type=F32)


def dot_t(left, right):
    return lax.dot_general(left, right, (((1,), (1,)), ((), ())), preferred_element_type=F32)


def split(value):
    high = value.astype(BF16)
    low = (value - high.astype(F32)).astype(BF16)
    return high, low


def column_of(row):
    return jnp.broadcast_to(row, (DH, row.shape[1])).T


def decay_tile(row, column, start_row, rows, start_col, cols):
    tile = jnp.broadcast_to(row[:, start_col : start_col + cols], (rows, cols))
    wide = jnp.concatenate([column[start_row : start_row + rows]] * (cols // DH), axis=1)
    gap = tile - wide
    if start_row + rows <= start_col:
        return jnp.exp(gap)
    key_pos = start_row + lax.broadcasted_iota(jnp.int32, (rows, cols), 0)
    query_pos = start_col + lax.broadcasted_iota(jnp.int32, (rows, cols), 1)
    return jnp.exp(jnp.where(key_pos <= query_pos, gap, -jnp.inf))


def pack_kernel(a_ref, b_ref, out_ref):
    count = out_ref.shape[0]
    width = a_ref.shape[1] // count
    for j in range(count):
        out_ref[j, :, :width] = a_ref[:, j * width : (j + 1) * width]
        out_ref[j, :, width:] = b_ref[:, j * width : (j + 1) * width]


def pack(a, b, count):
    rows, columns = a.shape
    return pl.pallas_call(
        pack_kernel,
        name="pack",
        out_shape=jax.ShapeDtypeStruct((count, rows, 2 * columns // count), a.dtype),
    )(a, b)


def unpack_kernel(in_ref, a_ref, b_ref):
    count = in_ref.shape[0]
    width = in_ref.shape[2] // 2
    for j in range(count):
        a_ref[:, j * width : (j + 1) * width] = in_ref[j, :, :width]
        b_ref[:, j * width : (j + 1) * width] = in_ref[j, :, width:]


def unpack(packed):
    count, rows, width = packed.shape
    shape = jax.ShapeDtypeStruct((rows, count * width // 2), packed.dtype)
    return pl.pallas_call(unpack_kernel, name="unpack", out_shape=(shape, shape))(packed)


def spread_kernel(in_ref, a_ref):
    count, _, width = in_ref.shape
    for j in range(count):
        a_ref[:, j * width : (j + 1) * width] = in_ref[j]


def spread(packed):
    count, rows, width = packed.shape
    shape = jax.ShapeDtypeStruct((rows, count * width), packed.dtype)
    return pl.pallas_call(spread_kernel, name="spread", out_shape=shape)(packed)


def gram_kernel(key_ref, value_ref, cumul_ref, out_ref, first_ref):
    block = pl.program_id(1)
    keys = key_ref[...]
    row = cumul_ref[0]
    last = row[:, SPAN - 1 :]
    weighted = keys.astype(F32).T * jnp.exp(last - row)
    high, low = split(weighted)
    both = jnp.concatenate([keys, value_ref[...]], axis=1)
    part = dot(high, both) + dot(low, both)
    pieces, piece = out_ref.shape[0], DH // out_ref.shape[0]

    @pl.when(block == 0)
    def _():
        first_ref[0] = part
        out_ref[:, :piece, :] = part.reshape(pieces, piece, 2 * DH)
        out_ref[:, piece:, :] = jnp.broadcast_to(last[None], (pieces, 8, 2 * DH))

    @pl.when(block == 1)
    def _():
        total = jnp.exp(last) * first_ref[0] + part
        out_ref[:, :piece, :] = total.reshape(pieces, piece, 2 * DH)
        out_ref[:, piece:, :] += jnp.broadcast_to(last[None], (pieces, 8, 2 * DH))


def scan_kernel(in_ref, out_ref, total_ref):
    number, piece = out_ref.shape[0], out_ref.shape[1]
    carry = jnp.zeros(out_ref.shape[1:], F32)
    for j in range(number):
        out_ref[j] = carry
        factor = jnp.exp(in_ref[j, piece:, :])
        total_ref[j] = factor
        carry = factor[:1] * carry + in_ref[j, :piece, :]


def scan_back_kernel(in_ref, total_ref, out_ref):
    carry = jnp.zeros(out_ref.shape[1:], F32)
    for j in reversed(range(out_ref.shape[0])):
        out_ref[j] = carry
        carry = total_ref[j, :1, :] * carry + in_ref[j]


def solve_kernel(
    key_ref,
    value_ref,
    query_ref,
    grad_ref,
    cumul_ref,
    ridge_ref,
    state_ref,
    first_ref,
    adjoint_ref,
    solved_ref,
    delta_ref,
    second_ref,
    early,
    late,
    stream,
    keys_t,
    weights,
    solution,
    residual,
    direction,
):
    head, block = pl.program_id(0), pl.program_id(1)
    keys, values, grads = key_ref[...], value_ref[...], grad_ref[...]
    row = cumul_ref[0, pl.ds(block, 1), :]
    first_total = cumul_ref[0, 0:1, SPAN - 1 :]
    column = column_of(row)
    start_decay = jnp.exp(row)
    ridge = ridge_ref[head]

    early[...] = decay_tile(row, column, 0, HALF, 0, HALF)
    late[:HALF] = decay_tile(row, column, HALF, HALF, HALF, HALF)
    late[HALF:] = decay_tile(row, column, 0, HALF, HALF, HALF)

    is_late = block == 1
    entry = jnp.where(is_late, jnp.exp(first_total), 1.0)
    local = jnp.where(is_late, 1.0, 0.0)
    state = entry * state_ref[...] + local * first_ref[0]
    gram_high, gram_low = split(state[:, :DH])
    value_high, value_low = split(state[:, DH:])
    zero = jnp.zeros((HALF, DH), BF16)
    stream[0:HALF] = jnp.concatenate([keys[HALF:], zero], axis=1)
    stream[HALF:SPAN] = jnp.concatenate([keys[:HALF], zero], axis=1)
    stream[SPAN : SPAN + DH] = jnp.concatenate([gram_high, gram_high], axis=1)
    stream[SPAN + DH :] = jnp.concatenate([gram_low, gram_low], axis=1)
    key_t = keys.astype(F32).T.astype(BF16)
    keys_t[:, :HALF] = key_t[:, HALF:]
    keys_t[:, HALF:] = key_t[:, :HALF]

    def starts(which, half, rhs):
        cols = slice(half * HALF, (half + 1) * HALF)
        solution[which, :, cols] = jnp.zeros((DH, HALF), F32)
        residual[which, :, cols] = rhs
        direction[which, :, cols] = rhs
        high, low = split(rhs)
        weights[which, :DH, cols] = high
        weights[which, DH:, cols] = low
        return jnp.sum(rhs * rhs, axis=0, keepdims=True)

    query_t = query_ref[...].astype(F32).T
    value_rows = jnp.concatenate([value_high, value_low], axis=0)
    rhos = [starts(0, half, query_t[:, half * HALF : (half + 1) * HALF]) for half in range(2)]
    for half in range(2):
        cols = slice(half * HALF, (half + 1) * HALF)
        grad_half = grads[cols]
        seen = dot_t(value_rows, grad_half)
        rhs = start_decay[:, cols] * (seen[:DH] + seen[DH:])
        if half == 0:
            masked = (early[...] * dot_t(values[:HALF], grad_half)).astype(BF16)
            rhs = rhs + dot(keys_t[:, HALF:], masked)
        else:
            turned = jnp.concatenate([values[HALF:], values[:HALF]], axis=0)
            masked = (late[...] * dot_t(turned, grad_half)).astype(BF16)
            rhs = rhs + dot(keys_t[...], masked)
        rhos.append(starts(1, half, rhs))

    def sweep(_, rhos):
        later = []
        for which in range(2):
            for half in range(2):
                cols = slice(half * HALF, (half + 1) * HALF)
                rho = rhos[2 * which + half]
                weight = weights[which, :, cols]
                if half == 0:
                    seen = dot(stream[HALF:], weight)
                    scores = (early[...] * seen[:HALF]).astype(BF16)
                    image = dot(keys_t[:, HALF:], scores)
                    gram = seen[HALF : HALF + DH] + seen[HALF + DH :]
                else:
                    seen = dot(stream[...], weight)
                    scores = (late[...] * seen[:SPAN]).astype(BF16)
                    image = dot(keys_t[...], scores)
                    gram = seen[SPAN : SPAN + DH] + seen[SPAN + DH :]
                way = direction[which, :, cols]
                image = image + start_decay[:, cols] * gram + ridge * way
                step = rho / (jnp.sum(way * image, axis=0, keepdims=True) + EPSILON)
                solution[which, :, cols] += step * way
                rest = residual[which, :, cols] - step * image
                residual[which, :, cols] = rest
                rho_next = jnp.sum(rest * rest, axis=0, keepdims=True)
                way = rest + rho_next / (rho + EPSILON) * way
                direction[which, :, cols] = way
                high, low = split(way)
                weights[which, :DH, cols] = high
                weights[which, DH:, cols] = low
                later.append(rho_next)
        return tuple(later)

    lax.fori_loop(0, SOLVE_STEPS, sweep, tuple(rhos))

    solved_t = solution[0]
    adjoint = solution[1].T.astype(BF16)
    adjoint_ref[...] = adjoint
    solved_ref[...] = solved_t.T.astype(BF16)
    high, low = split(start_decay * solved_t)
    both = jnp.concatenate([grads, -adjoint], axis=1)
    back = dot(high, both) + dot(low, both)

    @pl.when(block == 0)
    def _():
        delta_ref[...] = back

    @pl.when(block == 1)
    def _():
        delta_ref[...] += jnp.exp(first_total) * back
        second_ref[0] = back


def local_kernel(key_ref, value_ref, grad_ref, solved_ref, adjoint_ref, cumul_ref, key_out, value_out):
    block = pl.program_id(1)
    keys, values, grads = key_ref[...], value_ref[...], grad_ref[...]
    solved, adjoint = solved_ref[...], adjoint_ref[...]
    row = cumul_ref[0, pl.ds(block, 1), :]
    column = column_of(row)
    left = jnp.concatenate([values, keys], axis=1)
    right = jnp.concatenate([grads, -adjoint], axis=1)
    both = jnp.concatenate([grads, adjoint], axis=1)
    for half in range(2):
        mine = slice(half * HALF, (half + 1) * HALF)
        after = slice(half * HALF, SPAN)
        within = decay_tile(row, column, half * HALF, HALF, half * HALF, SPAN - half * HALF)
        along_solved = (within * dot_t(keys[mine], solved[after])).astype(BF16)
        along = (within * dot_t(left[mine], right[after])).astype(BF16)
        seen = dot(along_solved, both[after])
        value_out[mine] = seen[:, :DH]
        key_out[mine] = dot(along, solved[after]) - seen[:, DH:]


def final_kernel(key_ref, value_ref, state_ref, second_ref, cumul_ref, key_local, value_local, out_ref):
    block, head = pl.program_id(0), pl.program_id(1)
    row = cumul_ref[0, pl.ds(block, 1), :]
    last = cumul_ref[0, 1:2, SPAN - 1 :]
    weight = column_of(jnp.exp(row[:, SPAN - 1 :] - row))
    is_early = block == 0
    entry = jnp.where(is_early, jnp.exp(last), 1.0)
    local = jnp.where(is_early, 1.0, 0.0)
    state = entry * state_ref[...] + local * second_ref[0]
    value_t, gram = state[:, :DH], state[:, DH:]
    upper = jnp.concatenate([value_t, gram + gram.T], axis=1)
    lower = jnp.concatenate([jnp.zeros((DH, DH), F32), value_t.T], axis=1)
    high, low = split(jnp.concatenate([upper, lower], axis=0))
    both = jnp.concatenate([key_ref[...], value_ref[...]], axis=1)
    seen = dot(both, high) + dot(both, low)
    key_part = (key_local[...] + weight * seen[:, DH:]).astype(BF16)
    value_part = (value_local[...] + weight * seen[:, :DH]).astype(BF16)

    @pl.when(head == 0)
    def _():
        out_ref[:, :DH] = key_part
        out_ref[:, 2 * DH : 3 * DH] = value_part

    @pl.when(head == 1)
    def _():
        out_ref[:, DH : 2 * DH] = key_part
        out_ref[:, 3 * DH :] = value_part


def swap(pieces, axis):
    return lax.all_to_all(pieces, axis, split_axis=0, concat_axis=0, tiled=True)


def shards(queries, keys, values, grads_out, log_decay, ridge):
    heads = lax.axis_size("head")
    number = lax.axis_size("ctx")
    head_dev = log_decay.shape[0]
    tokens = log_decay.shape[1]
    count = tokens // SPAN
    piece = head_dev * DH // number
    grid = (head_dev, count)
    params = pltpu.CompilerParams(dimension_semantics=("arbitrary", "arbitrary"))

    first = swap(pack(keys, values, heads), "head").reshape(tokens, 2 * head_dev * DH)
    second = swap(pack(queries, grads_out, heads), "head").reshape(tokens, 2 * head_dev * DH)
    cumul = jnp.cumsum(log_decay.reshape(head_dev, count, SPAN), axis=2)

    low_spec = pl.BlockSpec((SPAN, DH), lambda h, b: (b, h))
    high_spec = pl.BlockSpec((SPAN, DH), lambda h, b: (b, head_dev + h))
    cumul_spec = pl.BlockSpec((1, count, SPAN), lambda h, b: (h, 0, 0))
    state_spec = pl.BlockSpec((DH, 2 * DH), lambda h, b: (h, 0))
    local_spec = pl.BlockSpec((1, DH, 2 * DH), lambda h, b: (h, 0, 0))
    state_shape = jax.ShapeDtypeStruct((head_dev * DH, 2 * DH), F32)
    local_shape = jax.ShapeDtypeStruct((head_dev, DH, 2 * DH), F32)

    out, first_state = pl.pallas_call(
        gram_kernel,
        name="gram",
        grid=grid,
        in_specs=[
            low_spec,
            high_spec,
            pl.BlockSpec((1, 1, SPAN), lambda h, b: (h * count + b, 0, 0)),
        ],
        out_specs=[
            pl.BlockSpec((number // head_dev, piece + 8, 2 * DH), lambda h, b: (h, 0, 0)),
            local_spec,
        ],
        out_shape=[jax.ShapeDtypeStruct((number, piece + 8, 2 * DH), F32), local_shape],
        compiler_params=params,
    )(first, first, cumul.reshape(head_dev * count, 1, SPAN))
    prefix, factors = pl.pallas_call(
        scan_kernel,
        name="scan",
        out_shape=(
            jax.ShapeDtypeStruct((number, piece, 2 * DH), F32),
            jax.ShapeDtypeStruct((number, 8, 2 * DH), F32),
        ),
    )(swap(out, "ctx"))
    state = swap(prefix, "ctx").reshape(head_dev * DH, 2 * DH)

    adjoint, solved, delta, second_state = pl.pallas_call(
        solve_kernel,
        name="solve",
        grid=grid,
        in_specs=[
            low_spec,
            high_spec,
            low_spec,
            high_spec,
            cumul_spec,
            pl.BlockSpec(memory_space=pltpu.SMEM),
            state_spec,
            local_spec,
        ],
        out_specs=[low_spec, low_spec, state_spec, local_spec],
        out_shape=[
            jax.ShapeDtypeStruct((tokens, head_dev * DH), BF16),
            jax.ShapeDtypeStruct((tokens, head_dev * DH), BF16),
            state_shape,
            local_shape,
        ],
        scratch_shapes=[
            pltpu.VMEM((HALF, HALF), F32),
            pltpu.VMEM((SPAN, HALF), F32),
            pltpu.VMEM((SPAN + 2 * DH, 2 * DH), BF16),
            pltpu.VMEM((DH, SPAN), BF16),
            pltpu.VMEM((2, 2 * DH, SPAN), BF16),
            pltpu.VMEM((2, DH, SPAN), F32),
            pltpu.VMEM((2, DH, SPAN), F32),
            pltpu.VMEM((2, DH, SPAN), F32),
        ],
        compiler_params=params,
    )(first, first, second, second, cumul, ridge, state, first_state)

    grad_queries = spread(swap(adjoint.reshape(heads, tokens // heads, head_dev * DH), "head"))

    key_local, value_local = pl.pallas_call(
        local_kernel,
        name="local",
        grid=grid,
        in_specs=[low_spec, high_spec, high_spec, low_spec, low_spec, cumul_spec],
        out_specs=[low_spec, low_spec],
        out_shape=[jax.ShapeDtypeStruct((tokens, head_dev * DH), F32)] * 2,
        compiler_params=params,
    )(first, first, second, solved, adjoint, cumul)

    suffix = pl.pallas_call(
        scan_back_kernel,
        name="scan_back",
        out_shape=jax.ShapeDtypeStruct((number, piece, 2 * DH), F32),
    )(swap(delta.reshape(number, piece, 2 * DH), "ctx"), factors)
    state_after = swap(suffix, "ctx").reshape(head_dev * DH, 2 * DH)

    def turned(spec):
        return pl.BlockSpec(spec.block_shape, lambda b, h: spec.index_map(h, b))

    grads = pl.pallas_call(
        final_kernel,
        name="final",
        grid=(count, head_dev),
        in_specs=[
            turned(spec)
            for spec in (
                low_spec,
                high_spec,
                state_spec,
                local_spec,
                cumul_spec,
                low_spec,
                low_spec,
            )
        ],
        out_specs=pl.BlockSpec((SPAN, 2 * head_dev * DH), lambda b, h: (b, 0)),
        out_shape=jax.ShapeDtypeStruct((tokens, 2 * head_dev * DH), BF16),
        compiler_params=params,
    )(first, first, state_after, second_state, cumul, key_local, value_local)
    grads = swap(grads.reshape(heads, tokens // heads, 2 * head_dev * DH), "head")
    grad_keys, grad_values = unpack(grads)
    return (grad_queries, grad_keys, grad_values)


def solution(mesh):
    return jax.shard_map(
        shards,
        mesh=mesh,
        in_specs=(
            P(("ctx", "head"), None),
            P(("ctx", "head"), None),
            P(("ctx", "head"), None),
            P(("ctx", "head"), None),
            P("head", "ctx"),
            P("head"),
        ),
        out_specs=(P(("ctx", "head"), None), P(("ctx", "head"), None), P(("ctx", "head"), None)),
        check_vma=False,
    )
```

```python
import jax
import jax.numpy as jnp
from jax import lax
from jax.experimental import pallas as pl
from jax.experimental.pallas import tpu as pltpu
from jax.sharding import PartitionSpec as P


DH = 128
SPAN = 512
HALF = SPAN // 2
SOLVE_STEPS = 8
EPSILON = 1e-06


F32 = jnp.float32
BF16 = jnp.bfloat16


MIB = 1 << 20


def grant(mib, **options):
    return pltpu.CompilerParams(vmem_limit_bytes=mib * MIB, **options)


def in_hbm(array):
    return pltpu.with_memory_space_constraint(array, pltpu.HBM)


def dot(left, right):
    return jnp.dot(left, right, preferred_element_type=F32)


def dot_t(left, right):
    return lax.dot_general(left, right, (((1,), (1,)), ((), ())), preferred_element_type=F32)


def split(value):
    high = value.astype(BF16)
    low = (value - high.astype(F32)).astype(BF16)
    return high, low


def column_of(row):
    return jnp.broadcast_to(row, (DH, row.shape[1])).T


def decay_tile(row, column, start_row, rows, start_col, cols):
    tile = jnp.broadcast_to(row[:, start_col : start_col + cols], (rows, cols))
    wide = jnp.concatenate([column[start_row : start_row + rows]] * (cols // DH), axis=1)
    gap = tile - wide
    if start_row + rows <= start_col:
        return jnp.exp(gap)
    key_pos = start_row + lax.broadcasted_iota(jnp.int32, (rows, cols), 0)
    query_pos = start_col + lax.broadcasted_iota(jnp.int32, (rows, cols), 1)
    return jnp.exp(jnp.where(key_pos <= query_pos, gap, -jnp.inf))


def pack_kernel(a_ref, b_ref, out_ref):
    count = out_ref.shape[0]
    width = a_ref.shape[1] // count
    for j in range(count):
        out_ref[j, :, :width] = a_ref[:, j * width : (j + 1) * width]
        out_ref[j, :, width:] = b_ref[:, j * width : (j + 1) * width]


def pack(a, b, count):
    rows, columns = a.shape
    return pl.pallas_call(
        pack_kernel,
        name="pack",
        out_shape=jax.ShapeDtypeStruct((count, rows, 2 * columns // count), a.dtype),
    )(a, b)


def parts_kernel(own_ref, a_ref, b_ref, *outs):
    width = a_ref.shape[1] // len(outs)
    for d, out_ref in enumerate(outs):
        cols = pl.ds(pl.multiple_of((own_ref[0] ^ d) * width, width), width)
        out_ref[:, :width] = a_ref[:, cols]
        out_ref[:, width:] = b_ref[:, cols]


def column_parts(own, a, b, count):
    rows, columns = a.shape
    return pl.pallas_call(
        parts_kernel,
        name="column_parts",
        compiler_params=grant(4),
        in_specs=[pl.BlockSpec(memory_space=pltpu.SMEM)] + [pl.BlockSpec(memory_space=pltpu.VMEM)] * 2,
        out_shape=[jax.ShapeDtypeStruct((rows, 2 * columns // count), a.dtype)] * count,
    )(own, a, b)


def rows_kernel(own_ref, a_ref, *outs):
    rows = a_ref.shape[0] // len(outs)
    for d, out_ref in enumerate(outs):
        out_ref[...] = a_ref[pl.ds(pl.multiple_of((own_ref[0] ^ d) * rows, rows), rows), :]


def row_parts(own, a, count):
    rows, columns = a.shape
    return pl.pallas_call(
        rows_kernel,
        name="row_parts",
        compiler_params=grant(3),
        in_specs=[pl.BlockSpec(memory_space=pltpu.SMEM), pl.BlockSpec(memory_space=pltpu.VMEM)],
        out_shape=[jax.ShapeDtypeStruct((rows // count, columns), a.dtype)] * count,
    )(own, a)


def trade(parts, axis):
    count = len(parts)
    out = [parts[0]]
    for d in range(1, count):
        out.append(lax.ppermute(parts[d], axis, [(i, i ^ d) for i in range(count)]))
    return out


def unpack_kernel(in_ref, a_ref, b_ref):
    count = in_ref.shape[0]
    width = in_ref.shape[2] // 2
    for j in range(count):
        a_ref[:, j * width : (j + 1) * width] = in_ref[j, :, :width]
        b_ref[:, j * width : (j + 1) * width] = in_ref[j, :, width:]


def unpack(packed):
    count, rows, width = packed.shape
    shape = jax.ShapeDtypeStruct((rows, count * width // 2), packed.dtype)
    return pl.pallas_call(unpack_kernel, name="unpack", compiler_params=grant(4), out_shape=(shape, shape))(packed)


def spread_kernel(own_ref, *refs):
    out_ref = refs[-1]
    for d, in_ref in enumerate(refs[:-1]):
        width = in_ref.shape[1]
        out_ref[:, pl.ds(pl.multiple_of((own_ref[0] ^ d) * width, width), width)] = in_ref[...]


def spread(own, parts):
    rows, width = parts[0].shape
    return pl.pallas_call(
        spread_kernel,
        name="spread",
        compiler_params=grant(3),
        in_specs=[pl.BlockSpec(memory_space=pltpu.SMEM)]
        + [pl.BlockSpec(memory_space=pltpu.VMEM)] * len(parts),
        out_shape=jax.ShapeDtypeStruct((rows, len(parts) * width), parts[0].dtype),
    )(own, *parts)


def gram_kernel(key_ref, value_ref, cumul_ref, out_ref, first_ref):
    block = pl.program_id(1)
    keys = key_ref[...]
    row = cumul_ref[0]
    last = row[:, SPAN - 1 :]
    weighted = keys.astype(F32).T * jnp.exp(last - row)
    high, low = split(weighted)
    both = jnp.concatenate([keys, value_ref[...]], axis=1)
    part = dot(high, both) + dot(low, both)
    pieces, piece = out_ref.shape[0], DH // out_ref.shape[0]

    @pl.when(block == 0)
    def _():
        first_ref[0] = part
        out_ref[:, :piece, :] = part.reshape(pieces, piece, 2 * DH)
        out_ref[:, piece:, :] = jnp.broadcast_to(last[None], (pieces, 8, 2 * DH))

    @pl.when(block == 1)
    def _():
        total = jnp.exp(last) * first_ref[0] + part
        out_ref[:, :piece, :] = total.reshape(pieces, piece, 2 * DH)
        out_ref[:, piece:, :] += jnp.broadcast_to(last[None], (pieces, 8, 2 * DH))


def scan_kernel(in_ref, out_ref, total_ref):
    number, piece = out_ref.shape[0], out_ref.shape[1]
    carry = jnp.zeros(out_ref.shape[1:], F32)
    for j in range(number):
        out_ref[j] = carry
        factor = jnp.exp(in_ref[j, piece:, :])
        total_ref[j] = factor
        carry = factor[:1] * carry + in_ref[j, :piece, :]


def scan_back_kernel(in_ref, total_ref, out_ref):
    carry = jnp.zeros(out_ref.shape[1:], F32)
    for j in reversed(range(out_ref.shape[0])):
        out_ref[j] = carry
        carry = total_ref[j, :1, :] * carry + in_ref[j]


def solve_kernel(
    own_ref,
    key_ref,
    value_ref,
    cumul_ref,
    ridge_ref,
    state_ref,
    first_ref,
    *rest,
):
    parts, rest = rest[:8], rest[8:]
    adjoint_ref, solved_ref, grad_ref, delta_ref, second_ref = rest[:5]
    early, late, stream, keys_t, weights, solution, residual, direction, images, gathered, sems = rest[5:]
    head, block = pl.program_id(0), pl.program_id(1)
    count = len(parts)
    copies = []
    for d in range(count):
        start = pl.multiple_of((own_ref[0] ^ d) * parts[d].shape[0], parts[d].shape[0])
        target = gathered.at[pl.ds(start, parts[d].shape[0]), :]
        copies.append(pltpu.make_async_copy(parts[d], target, sems.at[d]))
    is_first = jnp.logical_and(head == 0, block == 0)

    @pl.when(is_first)
    def _():
        for copy in copies:
            copy.start()

    keys, values = key_ref[...], value_ref[...]
    row = cumul_ref[0, pl.ds(block, 1), :]
    first_total = cumul_ref[0, 0:1, SPAN - 1 :]
    column = column_of(row)
    start_decay = jnp.exp(row)
    ridge = ridge_ref[head]

    early[...] = decay_tile(row, column, 0, HALF, 0, HALF)
    late[:HALF] = decay_tile(row, column, HALF, HALF, HALF, HALF)
    late[HALF:] = decay_tile(row, column, 0, HALF, HALF, HALF)

    is_late = block == 1
    entry = jnp.where(is_late, jnp.exp(first_total), 1.0)
    local = jnp.where(is_late, 1.0, 0.0)
    state = entry * state_ref[...] + local * first_ref[0]
    gram_high, gram_low = split(state[:, :DH])
    value_high, value_low = split(state[:, DH:])
    zero = jnp.zeros((HALF, DH), BF16)
    stream[0:HALF] = jnp.concatenate([keys[HALF:], zero], axis=1)
    stream[HALF:SPAN] = jnp.concatenate([keys[:HALF], zero], axis=1)
    stream[SPAN : SPAN + DH] = jnp.concatenate([gram_high, gram_high], axis=1)
    stream[SPAN + DH :] = jnp.concatenate([gram_low, gram_low], axis=1)
    key_t = keys.astype(F32).T.astype(BF16)
    keys_t[:, :HALF] = key_t[:, HALF:]
    keys_t[:, HALF:] = key_t[:, :HALF]

    @pl.when(is_first)
    def _():
        for copy in copies:
            copy.wait()

    rows = pl.ds(pl.multiple_of(block * SPAN, SPAN), SPAN)
    queries = gathered[rows, pl.ds(pl.multiple_of(head * DH, DH), DH)]
    grads = gathered[rows, pl.ds(pl.multiple_of((head + 2) * DH, DH), DH)]
    grad_ref[...] = grads

    query_t = queries.astype(F32).T
    value_rows = jnp.concatenate([value_high, value_low], axis=0)
    for half in range(2):
        cols = slice(half * HALF, (half + 1) * HALF)
        grad_half = grads[cols]
        seen = dot_t(value_rows, grad_half)
        rhs = start_decay[:, cols] * (seen[:DH] + seen[DH:])
        if half == 0:
            masked = (early[...] * dot_t(values[:HALF], grad_half)).astype(BF16)
            rhs = rhs + dot(keys_t[:, HALF:], masked)
        else:
            turned = jnp.concatenate([values[HALF:], values[:HALF]], axis=0)
            masked = (late[...] * dot_t(turned, grad_half)).astype(BF16)
            rhs = rhs + dot(keys_t[...], masked)
        both = jnp.concatenate([query_t[:, cols], rhs], axis=1)
        solution[half] = jnp.zeros((DH, SPAN), F32)
        residual[half] = both
        direction[half] = both
        high, low = split(both)
        weights[half, :DH] = high
        weights[half, DH:] = low

    chunks = [slice(c * DH, (c + 1) * DH) for c in range(SPAN // DH)]

    def norms(half):
        return tuple(
            jnp.sum(residual[half, :, c] * residual[half, :, c], axis=0, keepdims=True)
            for c in chunks
        )

    def multiply(half):
        weight = weights[half]
        tile, begin = (early, HALF) if half == 0 else (late, 0)
        count = SPAN - begin
        seen = dot(stream[begin:], weight)
        within = tile[...]
        scores = jnp.concatenate(
            [
                (within * seen[:count, :HALF]).astype(BF16),
                (within * seen[:count, HALF:]).astype(BF16),
            ],
            axis=1,
        )
        image = dot(keys_t[:, begin:], scores)
        gram = seen[count : count + DH] + seen[count + DH :]
        decay = start_decay[:, half * HALF : (half + 1) * HALF]
        images[half] = image + jnp.concatenate([decay, decay], axis=1) * gram

    def update(half, rhos, last=False):
        later = []
        for c, rho in zip(chunks, rhos):
            way = direction[half, :, c]
            image = images[half, :, c] + ridge * way
            step = rho / (jnp.sum(way * image, axis=0, keepdims=True) + EPSILON)
            solution[half, :, c] += step * way
            if last:
                continue
            left = residual[half, :, c] - step * image
            residual[half, :, c] = left
            rho_next = jnp.sum(left * left, axis=0, keepdims=True)
            way = left + rho_next / (rho + EPSILON) * way
            direction[half, :, c] = way
            high, low = split(way)
            weights[half, :DH, c] = high
            weights[half, DH:, c] = low
            later.append(rho_next)
        return tuple(later)

    multiply(0)

    def sweep(_, rhos):
        rho_early, rho_late = rhos
        multiply(1)
        rho_early = update(0, rho_early)
        multiply(0)
        rho_late = update(1, rho_late)
        return rho_early, rho_late

    rho_early, rho_late = lax.fori_loop(0, SOLVE_STEPS - 1, sweep, (norms(0), norms(1)))
    multiply(1)
    update(0, rho_early, True)
    update(1, rho_late, True)

    solved_t = jnp.concatenate([solution[0, :, :HALF], solution[1, :, :HALF]], axis=1)
    adjoint_t = jnp.concatenate([solution[0, :, HALF:], solution[1, :, HALF:]], axis=1)
    adjoint = adjoint_t.T.astype(BF16)
    adjoint_ref[...] = adjoint
    solved_ref[...] = solved_t.T.astype(BF16)
    high, low = split(start_decay * solved_t)
    both = jnp.concatenate([grads, -adjoint], axis=1)
    back = dot(high, both) + dot(low, both)

    @pl.when(block == 0)
    def _():
        delta_ref[...] = back

    @pl.when(block == 1)
    def _():
        delta_ref[...] += jnp.exp(first_total) * back
        second_ref[0] = back


def local_kernel(key_ref, value_ref, grad_ref, solved_ref, adjoint_ref, cumul_ref, key_out, value_out):
    block = pl.program_id(1)
    keys, values, grads = key_ref[...], value_ref[...], grad_ref[...]
    solved, adjoint = solved_ref[...], adjoint_ref[...]
    row = cumul_ref[0, pl.ds(block, 1), :]
    column = column_of(row)
    left = jnp.concatenate([values, keys], axis=1)
    right = jnp.concatenate([grads, -adjoint], axis=1)
    both = jnp.concatenate([grads, adjoint], axis=1)
    for half in range(2):
        mine = slice(half * HALF, (half + 1) * HALF)
        after = slice(half * HALF, SPAN)
        within = decay_tile(row, column, half * HALF, HALF, half * HALF, SPAN - half * HALF)
        along_solved = (within * dot_t(keys[mine], solved[after])).astype(BF16)
        along = (within * dot_t(left[mine], right[after])).astype(BF16)
        seen = dot(along_solved, both[after])
        value_out[mine] = seen[:, :DH]
        key_out[mine] = dot(along, solved[after]) - seen[:, DH:]


def final_kernel(key_ref, value_ref, state_ref, second_ref, cumul_ref, key_local, value_local, out_ref):
    block, head = pl.program_id(0), pl.program_id(1)
    row = cumul_ref[0, pl.ds(block, 1), :]
    last = cumul_ref[0, 1:2, SPAN - 1 :]
    weight = column_of(jnp.exp(row[:, SPAN - 1 :] - row))
    is_early = block == 0
    entry = jnp.where(is_early, jnp.exp(last), 1.0)
    local = jnp.where(is_early, 1.0, 0.0)
    state = entry * state_ref[...] + local * second_ref[0]
    value_t, gram = state[:, :DH], state[:, DH:]
    upper = jnp.concatenate([value_t, gram + gram.T], axis=1)
    lower = jnp.concatenate([jnp.zeros((DH, DH), F32), value_t.T], axis=1)
    high, low = split(jnp.concatenate([upper, lower], axis=0))
    both = jnp.concatenate([key_ref[...], value_ref[...]], axis=1)
    seen = dot(both, high) + dot(both, low)
    key_part = (key_local[...] + weight * seen[:, DH:]).astype(BF16)
    value_part = (value_local[...] + weight * seen[:, :DH]).astype(BF16)

    @pl.when(head == 0)
    def _():
        out_ref[:, :DH] = key_part
        out_ref[:, 2 * DH : 3 * DH] = value_part

    @pl.when(head == 1)
    def _():
        out_ref[:, DH : 2 * DH] = key_part
        out_ref[:, 3 * DH :] = value_part


def swap(pieces, axis):
    return lax.all_to_all(pieces, axis, split_axis=0, concat_axis=0, tiled=True)


def shards(queries, keys, values, grads_out, log_decay, ridge):
    heads = lax.axis_size("head")
    number = lax.axis_size("ctx")
    head_dev = log_decay.shape[0]
    tokens = log_decay.shape[1]
    count = tokens // SPAN
    piece = head_dev * DH // number
    grid = (head_dev, count)

    first = swap(pack(keys, values, heads), "head").reshape(tokens, 2 * head_dev * DH)
    own = lax.axis_index("head").astype(jnp.int32).reshape(1)
    parts = trade(column_parts(own, queries, grads_out, heads), "head")
    cumul = jnp.cumsum(log_decay.reshape(head_dev, count, SPAN), axis=2)

    low_spec = pl.BlockSpec((SPAN, DH), lambda h, b: (b, h))
    high_spec = pl.BlockSpec((SPAN, DH), lambda h, b: (b, head_dev + h))
    cumul_spec = pl.BlockSpec((1, count, SPAN), lambda h, b: (h, 0, 0))
    state_spec = pl.BlockSpec((DH, 2 * DH), lambda h, b: (h, 0))
    local_spec = pl.BlockSpec((1, DH, 2 * DH), lambda h, b: (h, 0, 0))
    state_shape = jax.ShapeDtypeStruct((head_dev * DH, 2 * DH), F32)
    local_hbm = pltpu.HBM((head_dev, DH, 2 * DH), F32)

    out, first_state = pl.pallas_call(
        gram_kernel,
        name="gram",
        grid=grid,
        in_specs=[
            low_spec,
            high_spec,
            pl.BlockSpec((1, 1, SPAN), lambda h, b: (h * count + b, 0, 0)),
        ],
        out_specs=[
            pl.BlockSpec((number // head_dev, piece + 8, 2 * DH), lambda h, b: (h, 0, 0)),
            local_spec,
        ],
        out_shape=[jax.ShapeDtypeStruct((number, piece + 8, 2 * DH), F32), local_hbm],
        compiler_params=grant(6),
    )(first, first, cumul.reshape(head_dev * count, 1, SPAN))
    prefix, factors = pl.pallas_call(
        scan_kernel,
        name="scan",
        compiler_params=grant(2),
        out_shape=(
            jax.ShapeDtypeStruct((number, piece, 2 * DH), F32),
            jax.ShapeDtypeStruct((number, 8, 2 * DH), F32),
        ),
    )(swap(out, "ctx"))
    state = swap(prefix, "ctx").reshape(head_dev * DH, 2 * DH)

    token_hbm = pltpu.HBM((tokens, head_dev * DH), BF16)
    adjoint, solved, grads_local, delta, second_state = pl.pallas_call(
        solve_kernel,
        name="solve",
        grid=grid,
        in_specs=[
            pl.BlockSpec(memory_space=pltpu.SMEM),
            low_spec,
            high_spec,
            cumul_spec,
            pl.BlockSpec(memory_space=pltpu.SMEM),
            state_spec,
            local_spec,
        ]
        + [pl.BlockSpec(memory_space=pl.ANY)] * heads,
        out_specs=[low_spec, low_spec, low_spec, state_spec, local_spec],
        out_shape=[token_hbm, token_hbm, token_hbm, state_shape, local_hbm],
        scratch_shapes=[
            pltpu.VMEM((HALF, HALF), F32),
            pltpu.VMEM((SPAN, HALF), F32),
            pltpu.VMEM((SPAN + 2 * DH, 2 * DH), BF16),
            pltpu.VMEM((DH, SPAN), BF16),
            pltpu.VMEM((2, 2 * DH, SPAN), BF16),
            pltpu.VMEM((2, DH, SPAN), F32),
            pltpu.VMEM((2, DH, SPAN), F32),
            pltpu.VMEM((2, DH, SPAN), F32),
            pltpu.VMEM((2, DH, SPAN), F32),
            pltpu.VMEM((tokens, 2 * head_dev * DH), BF16),
            pltpu.SemaphoreType.DMA((heads,)),
        ],
        compiler_params=grant(12),
    )(own, first, first, cumul, in_hbm(ridge), state, first_state, *parts)

    grad_queries = spread(own, trade(row_parts(own, adjoint, heads), "head"))

    key_local, value_local = pl.pallas_call(
        local_kernel,
        name="local",
        grid=grid,
        in_specs=[low_spec, high_spec, low_spec, low_spec, low_spec, cumul_spec],
        out_specs=[low_spec, low_spec],
        out_shape=[pltpu.HBM((tokens, head_dev * DH), F32)] * 2,
        compiler_params=grant(10),
    )(first, first, grads_local, solved, adjoint, cumul)

    suffix = pl.pallas_call(
        scan_back_kernel,
        name="scan_back",
        compiler_params=grant(2),
        out_shape=jax.ShapeDtypeStruct((number, piece, 2 * DH), F32),
    )(swap(delta.reshape(number, piece, 2 * DH), "ctx"), factors)
    state_after = swap(suffix, "ctx").reshape(head_dev * DH, 2 * DH)

    def turned(spec):
        return pl.BlockSpec(spec.block_shape, lambda b, h: spec.index_map(h, b))

    grads = pl.pallas_call(
        final_kernel,
        name="final",
        grid=(count, head_dev),
        in_specs=[
            turned(spec)
            for spec in (
                low_spec,
                high_spec,
                state_spec,
                local_spec,
                cumul_spec,
                low_spec,
                low_spec,
            )
        ],
        out_specs=pl.BlockSpec((SPAN, 2 * head_dev * DH), lambda b, h: (b, 0)),
        out_shape=jax.ShapeDtypeStruct((tokens, 2 * head_dev * DH), BF16),
        compiler_params=grant(10),
    )(first, first, state_after, second_state, cumul, in_hbm(key_local), in_hbm(value_local))
    grads = swap(grads.reshape(heads, tokens // heads, 2 * head_dev * DH), "head")
    grad_keys, grad_values = unpack(grads)
    return (grad_queries, grad_keys, grad_values)


def solution(mesh):
    return jax.shard_map(
        shards,
        mesh=mesh,
        in_specs=(
            P(("ctx", "head"), None),
            P(("ctx", "head"), None),
            P(("ctx", "head"), None),
            P(("ctx", "head"), None),
            P("head", "ctx"),
            P("head"),
        ),
        out_specs=(P(("ctx", "head"), None), P(("ctx", "head"), None), P(("ctx", "head"), None)),
        check_vma=False,
    )
```

```python
import jax
import jax.numpy as jnp
from jax import lax
from jax.experimental import pallas as pl
from jax.experimental.pallas import tpu as pltpu
from jax.sharding import PartitionSpec as P


DH = 128
SPAN = 512
HALF = SPAN // 2
SOLVE_STEPS = 8
EPSILON = 1e-06


F32 = jnp.float32
BF16 = jnp.bfloat16


MIB = 1 << 20


def grant(mib, **options):
    return pltpu.CompilerParams(vmem_limit_bytes=mib * MIB, **options)


def in_hbm(array):
    return pltpu.with_memory_space_constraint(array, pltpu.HBM)


def dot(left, right):
    return jnp.dot(left, right, preferred_element_type=F32)


def dot_t(left, right):
    return lax.dot_general(left, right, (((1,), (1,)), ((), ())), preferred_element_type=F32)


def split(value):
    high = value.astype(BF16)
    low = (value - high.astype(F32)).astype(BF16)
    return high, low


def column_of(row):
    return jnp.broadcast_to(row, (DH, row.shape[1])).T


def decay_tile(row, column, start_row, rows, start_col, cols):
    tile = jnp.broadcast_to(row[:, start_col : start_col + cols], (rows, cols))
    wide = jnp.concatenate([column[start_row : start_row + rows]] * (cols // DH), axis=1)
    gap = tile - wide
    if start_row + rows <= start_col:
        return jnp.exp(gap)
    key_pos = start_row + lax.broadcasted_iota(jnp.int32, (rows, cols), 0)
    query_pos = start_col + lax.broadcasted_iota(jnp.int32, (rows, cols), 1)
    return jnp.exp(jnp.where(key_pos <= query_pos, gap, -jnp.inf))


def pack_kernel(a_ref, b_ref, out_ref):
    count = out_ref.shape[0]
    width = a_ref.shape[1] // count
    for j in range(count):
        out_ref[j, :, :width] = a_ref[:, j * width : (j + 1) * width]
        out_ref[j, :, width:] = b_ref[:, j * width : (j + 1) * width]


def pack(a, b, count):
    rows, columns = a.shape
    return pl.pallas_call(
        pack_kernel,
        name="pack",
        out_shape=jax.ShapeDtypeStruct((count, rows, 2 * columns // count), a.dtype),
    )(a, b)


def parts_kernel(own_ref, a_ref, b_ref, *outs):
    width = a_ref.shape[1] // len(outs)
    for d, out_ref in enumerate(outs):
        cols = pl.ds(pl.multiple_of((own_ref[0] ^ d) * width, width), width)
        out_ref[:, :width] = a_ref[:, cols]
        out_ref[:, width:] = b_ref[:, cols]


def column_parts(own, a, b, count):
    rows, columns = a.shape
    return pl.pallas_call(
        parts_kernel,
        name="column_parts",
        compiler_params=grant(4),
        in_specs=[pl.BlockSpec(memory_space=pltpu.SMEM)] + [pl.BlockSpec(memory_space=pltpu.VMEM)] * 2,
        out_shape=[jax.ShapeDtypeStruct((rows, 2 * columns // count), a.dtype)] * count,
    )(own, a, b)


def rows_kernel(own_ref, a_ref, *outs):
    rows = a_ref.shape[0] // len(outs)
    for d, out_ref in enumerate(outs):
        out_ref[...] = a_ref[pl.ds(pl.multiple_of((own_ref[0] ^ d) * rows, rows), rows), :]


def row_parts(own, a, count):
    rows, columns = a.shape
    return pl.pallas_call(
        rows_kernel,
        name="row_parts",
        compiler_params=grant(3),
        in_specs=[pl.BlockSpec(memory_space=pltpu.SMEM), pl.BlockSpec(memory_space=pltpu.VMEM)],
        out_shape=[jax.ShapeDtypeStruct((rows // count, columns), a.dtype)] * count,
    )(own, a)


def trade(parts, axis):
    count = len(parts)
    out = [parts[0]]
    for d in range(1, count):
        out.append(lax.ppermute(parts[d], axis, [(i, i ^ d) for i in range(count)]))
    return out


def unpack_kernel(in_ref, a_ref, b_ref):
    count = in_ref.shape[0]
    width = in_ref.shape[2] // 2
    for j in range(count):
        a_ref[:, j * width : (j + 1) * width] = in_ref[j, :, :width]
        b_ref[:, j * width : (j + 1) * width] = in_ref[j, :, width:]


def unpack(packed):
    count, rows, width = packed.shape
    shape = jax.ShapeDtypeStruct((rows, count * width // 2), packed.dtype)
    return pl.pallas_call(unpack_kernel, name="unpack", compiler_params=grant(4), out_shape=(shape, shape))(packed)


def spread_kernel(own_ref, *refs):
    out_ref = refs[-1]
    for d, in_ref in enumerate(refs[:-1]):
        width = in_ref.shape[1]
        out_ref[:, pl.ds(pl.multiple_of((own_ref[0] ^ d) * width, width), width)] = in_ref[...]


def spread(own, parts):
    rows, width = parts[0].shape
    return pl.pallas_call(
        spread_kernel,
        name="spread",
        compiler_params=grant(3),
        in_specs=[pl.BlockSpec(memory_space=pltpu.SMEM)]
        + [pl.BlockSpec(memory_space=pltpu.VMEM)] * len(parts),
        out_shape=jax.ShapeDtypeStruct((rows, len(parts) * width), parts[0].dtype),
    )(own, *parts)


def gram_kernel(key_ref, value_ref, cumul_ref, out_ref, first_ref):
    block = pl.program_id(1)
    keys = key_ref[...]
    row = cumul_ref[0]
    last = row[:, SPAN - 1 :]
    weighted = keys.astype(F32).T * jnp.exp(last - row)
    high, low = split(weighted)
    both = jnp.concatenate([keys, value_ref[...]], axis=1)
    part = dot(high, both) + dot(low, both)
    pieces, piece = out_ref.shape[0], DH // out_ref.shape[0]

    @pl.when(block == 0)
    def _():
        first_ref[0] = part
        out_ref[:, :piece, :] = part.reshape(pieces, piece, 2 * DH)
        out_ref[:, piece:, :] = jnp.broadcast_to(last[None], (pieces, 8, 2 * DH))

    @pl.when(block == 1)
    def _():
        total = jnp.exp(last) * first_ref[0] + part
        out_ref[:, :piece, :] = total.reshape(pieces, piece, 2 * DH)
        out_ref[:, piece:, :] += jnp.broadcast_to(last[None], (pieces, 8, 2 * DH))


def scan_kernel(in_ref, out_ref, total_ref):
    number, piece = out_ref.shape[0], out_ref.shape[1]
    carry = jnp.zeros(out_ref.shape[1:], F32)
    for j in range(number):
        out_ref[j] = carry
        factor = jnp.exp(in_ref[j, piece:, :])
        total_ref[j] = factor
        carry = factor[:1] * carry + in_ref[j, :piece, :]


def scan_back_kernel(in_ref, total_ref, out_ref):
    carry = jnp.zeros(out_ref.shape[1:], F32)
    for j in reversed(range(out_ref.shape[0])):
        out_ref[j] = carry
        carry = total_ref[j, :1, :] * carry + in_ref[j]


def solve_kernel(
    own_ref,
    key_ref,
    value_ref,
    cumul_ref,
    ridge_ref,
    state_ref,
    first_ref,
    *rest,
):
    parts, rest = rest[:8], rest[8:]
    adjoint_ref, solved_ref, grad_ref, delta_ref, second_ref = rest[:5]
    early, late, stream, mixing, gathered = rest[5:10]
    weights, scaled, solution, residual, direction, images, rhos = zip(rest[10:17], rest[17:])
    head, block = pl.program_id(0), pl.program_id(1)
    count = len(parts)

    @pl.when(jnp.logical_and(head == 0, block == 0))
    def _():
        for d in range(count):
            size = parts[d].shape[0]
            start = pl.multiple_of((own_ref[0] ^ d) * size, size)
            gathered[pl.ds(start, size), :] = parts[d][...]

    keys, values = key_ref[...], value_ref[...]
    row = cumul_ref[0, pl.ds(block, 1), :]
    first_total = cumul_ref[0, 0:1, SPAN - 1 :]
    column = column_of(row)
    start_decay = jnp.exp(row)
    ridge = ridge_ref[head]

    early[...] = decay_tile(row, column, 0, HALF, 0, HALF)
    late[:HALF] = decay_tile(row, column, HALF, HALF, HALF, HALF)
    late[HALF:] = decay_tile(row, column, 0, HALF, HALF, HALF)

    is_late = block == 1
    entry = jnp.where(is_late, jnp.exp(first_total), 1.0)
    local = jnp.where(is_late, 1.0, 0.0)
    state = entry * state_ref[...] + local * first_ref[0]
    gram_high, gram_low = split(state[:, :DH])
    value_high, value_low = split(state[:, DH:])
    stream[:HALF] = keys[HALF:]
    stream[HALF:] = keys[:HALF]
    key_t = keys.astype(F32).T.astype(BF16)
    mixing[:, 3 * DH : 3 * DH + HALF] = key_t[:, HALF:]
    mixing[:, 3 * DH + HALF :] = key_t[:, :HALF]
    mixing[:, : 3 * DH] = jnp.concatenate([gram_high, gram_high, gram_low], axis=1)

    rows = pl.ds(pl.multiple_of(block * SPAN, SPAN), SPAN)
    queries = gathered[rows, pl.ds(pl.multiple_of(head * DH, DH), DH)]
    grads = gathered[rows, pl.ds(pl.multiple_of((head + 2) * DH, DH), DH)]
    grad_ref[...] = grads

    query_t = queries.astype(F32).T
    value_rows = jnp.concatenate([value_high, value_low], axis=0)
    for half in range(2):
        cols = slice(half * HALF, (half + 1) * HALF)
        grad_half = grads[cols]
        seen = dot_t(value_rows, grad_half)
        rhs = start_decay[:, cols] * (seen[:DH] + seen[DH:])
        if half == 0:
            masked = (early[...] * dot_t(values[:HALF], grad_half)).astype(BF16)
            rhs = rhs + dot(mixing[:, 3 * DH + HALF :], masked)
        else:
            turned = jnp.concatenate([values[HALF:], values[:HALF]], axis=0)
            masked = (late[...] * dot_t(turned, grad_half)).astype(BF16)
            rhs = rhs + dot(mixing[:, 3 * DH :], masked)
        both = jnp.concatenate([query_t[:, cols], rhs], axis=1)
        solution[half][...] = jnp.zeros((DH, SPAN), F32)
        residual[half][...] = both
        direction[half][...] = both
        decay = start_decay[:, cols]
        high, low = split(jnp.concatenate([decay, decay], axis=1) * both)
        weights[half][...] = both.astype(BF16)
        scaled[half][:DH] = high
        scaled[half][DH : 2 * DH] = low
        scaled[half][2 * DH :] = high

    groups = [slice(g * 16, (g + 1) * 16) for g in range(DH // 16)]

    def column_sum(parts):
        total = parts[0]
        for part in parts[1:]:
            total = total + part
        return jnp.sum(total, axis=0, keepdims=True)

    def norms(half):
        return column_sum([residual[half][g, :] * residual[half][g, :] for g in groups])

    def multiply(half):
        tile, begin = (early, HALF) if half == 0 else (late, 0)
        count = SPAN - begin
        seen = dot(stream[begin:], weights[half][...])
        yield
        scores = []
        for start in range(0, count, 16):
            within = tile[start : start + 16]
            part = seen[start : start + 16]
            scores.append(
                jnp.concatenate(
                    [
                        (within * part[:, :HALF]).astype(BF16),
                        (within * part[:, HALF:]).astype(BF16),
                    ],
                    axis=1,
                )
            )
            yield
        if half == 0:
            left = jnp.concatenate([mixing[:, : 3 * DH], mixing[:, 3 * DH + HALF :]], axis=1)
        else:
            left = mixing[...]
        images[half][...] = dot(left, jnp.concatenate([scaled[half][...]] + scores, axis=0))
        yield

    def update(half, last=False):
        rho = rhos[half][...]
        decay = start_decay[:, half * HALF : (half + 1) * HALF]
        decay = jnp.concatenate([decay, decay], axis=1)
        along = 0.0
        for g in groups:
            way = direction[half][g, :]
            image = images[half][g, :] + ridge * way
            images[half][g, :] = image
            along = along + way * image
            yield
        step = rho / (jnp.sum(along, axis=0, keepdims=True) + EPSILON)
        norm = 0.0
        for g in groups:
            solution[half][g, :] += step * direction[half][g, :]
            if not last:
                left = residual[half][g, :] - step * images[half][g, :]
                residual[half][g, :] = left
                norm = norm + left * left
            yield
        if last:
            return
        rho_next = jnp.sum(norm, axis=0, keepdims=True)
        rhos[half][...] = rho_next
        turn = rho_next / (rho + EPSILON)
        for g in groups:
            way = residual[half][g, :] + turn * direction[half][g, :]
            direction[half][g, :] = way
            weights[half][g, :] = way.astype(BF16)
            high, low = split(decay * way)
            scaled[half][g, :] = high
            scaled[half][DH + g.start : DH + g.stop, :] = low
            scaled[half][2 * DH + g.start : 2 * DH + g.stop, :] = high
            yield

    def weave(multiplying, updating, ratio):
        for _ in multiplying:
            for _ in range(ratio):
                next(updating, None)
        for _ in updating:
            pass

    for half in range(2):
        rhos[half][...] = norms(half)
    for _ in multiply(0):
        pass

    def sweep(_, carry):
        weave(multiply(1), update(0), 1)
        weave(multiply(0), update(1), 1)
        return carry

    lax.fori_loop(0, SOLVE_STEPS - 1, sweep, 0, unroll=True)
    weave(multiply(1), update(0, True), 1)
    for _ in update(1, True):
        pass

    solved_t = jnp.concatenate([solution[0][:, :HALF], solution[1][:, :HALF]], axis=1)
    adjoint_t = jnp.concatenate([solution[0][:, HALF:], solution[1][:, HALF:]], axis=1)
    adjoint = adjoint_t.T.astype(BF16)
    adjoint_ref[...] = adjoint
    solved_ref[...] = solved_t.T.astype(BF16)
    high, low = split(start_decay * solved_t)
    both = jnp.concatenate([grads, -adjoint], axis=1)
    back = dot(high, both) + dot(low, both)

    @pl.when(block == 0)
    def _():
        delta_ref[...] = back

    @pl.when(block == 1)
    def _():
        delta_ref[...] += jnp.exp(first_total) * back
        second_ref[0] = back


def local_kernel(key_ref, value_ref, grad_ref, solved_ref, adjoint_ref, cumul_ref, key_out, value_out):
    block = pl.program_id(1)
    keys, values, grads = key_ref[...], value_ref[...], grad_ref[...]
    solved, adjoint = solved_ref[...], adjoint_ref[...]
    row = cumul_ref[0, pl.ds(block, 1), :]
    column = column_of(row)
    left = jnp.concatenate([values, keys], axis=1)
    right = jnp.concatenate([grads, -adjoint], axis=1)
    both = jnp.concatenate([grads, adjoint], axis=1)
    for half in range(2):
        mine = slice(half * HALF, (half + 1) * HALF)
        after = slice(half * HALF, SPAN)
        within = decay_tile(row, column, half * HALF, HALF, half * HALF, SPAN - half * HALF)
        along_solved = (within * dot_t(keys[mine], solved[after])).astype(BF16)
        along = (within * dot_t(left[mine], right[after])).astype(BF16)
        seen = dot(along_solved, both[after])
        value_out[mine] = seen[:, :DH]
        key_out[mine] = dot(along, solved[after]) - seen[:, DH:]


def final_kernel(key_ref, value_ref, state_ref, second_ref, cumul_ref, key_local, value_local, out_ref):
    block, head = pl.program_id(0), pl.program_id(1)
    row = cumul_ref[0, pl.ds(block, 1), :]
    last = cumul_ref[0, 1:2, SPAN - 1 :]
    weight = column_of(jnp.exp(row[:, SPAN - 1 :] - row))
    is_early = block == 0
    entry = jnp.where(is_early, jnp.exp(last), 1.0)
    local = jnp.where(is_early, 1.0, 0.0)
    state = entry * state_ref[...] + local * second_ref[0]
    value_t, gram = state[:, :DH], state[:, DH:]
    upper = jnp.concatenate([value_t, gram + gram.T], axis=1)
    lower = jnp.concatenate([jnp.zeros((DH, DH), F32), value_t.T], axis=1)
    high, low = split(jnp.concatenate([upper, lower], axis=0))
    both = jnp.concatenate([key_ref[...], value_ref[...]], axis=1)
    seen = dot(both, high) + dot(both, low)
    key_part = (key_local[...] + weight * seen[:, DH:]).astype(BF16)
    value_part = (value_local[...] + weight * seen[:, :DH]).astype(BF16)

    @pl.when(head == 0)
    def _():
        out_ref[:, :DH] = key_part
        out_ref[:, 2 * DH : 3 * DH] = value_part

    @pl.when(head == 1)
    def _():
        out_ref[:, DH : 2 * DH] = key_part
        out_ref[:, 3 * DH :] = value_part


def swap(pieces, axis):
    return lax.all_to_all(pieces, axis, split_axis=0, concat_axis=0, tiled=True)


def shards(queries, keys, values, grads_out, log_decay, ridge):
    heads = lax.axis_size("head")
    number = lax.axis_size("ctx")
    head_dev = log_decay.shape[0]
    tokens = log_decay.shape[1]
    count = tokens // SPAN
    piece = head_dev * DH // number
    grid = (head_dev, count)

    first = swap(pack(keys, values, heads), "head").reshape(tokens, 2 * head_dev * DH)
    own = lax.axis_index("head").astype(jnp.int32).reshape(1)
    parts = trade(column_parts(own, queries, grads_out, heads), "head")
    cumul = jnp.cumsum(log_decay.reshape(head_dev, count, SPAN), axis=2)

    low_spec = pl.BlockSpec((SPAN, DH), lambda h, b: (b, h))
    high_spec = pl.BlockSpec((SPAN, DH), lambda h, b: (b, head_dev + h))
    cumul_spec = pl.BlockSpec((1, count, SPAN), lambda h, b: (h, 0, 0))
    state_spec = pl.BlockSpec((DH, 2 * DH), lambda h, b: (h, 0))
    local_spec = pl.BlockSpec((1, DH, 2 * DH), lambda h, b: (h, 0, 0))
    state_shape = jax.ShapeDtypeStruct((head_dev * DH, 2 * DH), F32)
    local_hbm = pltpu.HBM((head_dev, DH, 2 * DH), F32)

    out, first_state = pl.pallas_call(
        gram_kernel,
        name="gram",
        grid=grid,
        in_specs=[
            low_spec,
            high_spec,
            pl.BlockSpec((1, 1, SPAN), lambda h, b: (h * count + b, 0, 0)),
        ],
        out_specs=[
            pl.BlockSpec((number // head_dev, piece + 8, 2 * DH), lambda h, b: (h, 0, 0)),
            local_spec,
        ],
        out_shape=[jax.ShapeDtypeStruct((number, piece + 8, 2 * DH), F32), local_hbm],
        compiler_params=grant(6),
    )(first, first, cumul.reshape(head_dev * count, 1, SPAN))
    prefix, factors = pl.pallas_call(
        scan_kernel,
        name="scan",
        compiler_params=grant(2),
        out_shape=(
            jax.ShapeDtypeStruct((number, piece, 2 * DH), F32),
            jax.ShapeDtypeStruct((number, 8, 2 * DH), F32),
        ),
    )(swap(out, "ctx"))
    state = swap(prefix, "ctx").reshape(head_dev * DH, 2 * DH)

    token_hbm = pltpu.HBM((tokens, head_dev * DH), BF16)
    adjoint, solved, grads_local, delta, second_state = pl.pallas_call(
        solve_kernel,
        name="solve",
        grid=grid,
        in_specs=[
            pl.BlockSpec(memory_space=pltpu.SMEM),
            low_spec,
            high_spec,
            cumul_spec,
            pl.BlockSpec(memory_space=pltpu.SMEM),
            state_spec,
            local_spec,
        ]
        + [pl.BlockSpec(memory_space=pltpu.VMEM)] * heads,
        out_specs=[low_spec, low_spec, low_spec, state_spec, local_spec],
        out_shape=[token_hbm, token_hbm, token_hbm, state_shape, local_hbm],
        scratch_shapes=[
            pltpu.VMEM((HALF, HALF), F32),
            pltpu.VMEM((SPAN, HALF), F32),
            pltpu.VMEM((SPAN, DH), BF16),
            pltpu.VMEM((DH, SPAN + 3 * DH), BF16),
            pltpu.VMEM((tokens, 2 * head_dev * DH), BF16),
        ]
        + [
            pltpu.VMEM((DH, SPAN), BF16),
            pltpu.VMEM((3 * DH, SPAN), BF16),
            pltpu.VMEM((DH, SPAN), F32),
            pltpu.VMEM((DH, SPAN), F32),
            pltpu.VMEM((DH, SPAN), F32),
            pltpu.VMEM((DH, SPAN), F32),
            pltpu.VMEM((1, SPAN), F32),
        ]
        * 2,
        compiler_params=grant(12),
    )(own, first, first, cumul, in_hbm(ridge), state, first_state, *parts)

    grad_queries = spread(own, trade(row_parts(own, adjoint, heads), "head"))

    key_local, value_local = pl.pallas_call(
        local_kernel,
        name="local",
        grid=grid,
        in_specs=[low_spec, high_spec, low_spec, low_spec, low_spec, cumul_spec],
        out_specs=[low_spec, low_spec],
        out_shape=[pltpu.HBM((tokens, head_dev * DH), F32)] * 2,
        compiler_params=grant(10),
    )(first, first, grads_local, solved, adjoint, cumul)

    suffix = pl.pallas_call(
        scan_back_kernel,
        name="scan_back",
        compiler_params=grant(2),
        out_shape=jax.ShapeDtypeStruct((number, piece, 2 * DH), F32),
    )(swap(delta.reshape(number, piece, 2 * DH), "ctx"), factors)
    state_after = swap(suffix, "ctx").reshape(head_dev * DH, 2 * DH)

    def turned(spec):
        return pl.BlockSpec(spec.block_shape, lambda b, h: spec.index_map(h, b))

    grads = pl.pallas_call(
        final_kernel,
        name="final",
        grid=(count, head_dev),
        in_specs=[
            turned(spec)
            for spec in (
                low_spec,
                high_spec,
                state_spec,
                local_spec,
                cumul_spec,
                low_spec,
                low_spec,
            )
        ],
        out_specs=pl.BlockSpec((SPAN, 2 * head_dev * DH), lambda b, h: (b, 0)),
        out_shape=jax.ShapeDtypeStruct((tokens, 2 * head_dev * DH), BF16),
        compiler_params=grant(10),
    )(first, first, state_after, second_state, cumul, in_hbm(key_local), in_hbm(value_local))
    grads = swap(grads.reshape(heads, tokens // heads, 2 * head_dev * DH), "head")
    grad_keys, grad_values = unpack(grads)
    return (grad_queries, grad_keys, grad_values)


def solution(mesh):
    return jax.shard_map(
        shards,
        mesh=mesh,
        in_specs=(
            P(("ctx", "head"), None),
            P(("ctx", "head"), None),
            P(("ctx", "head"), None),
            P(("ctx", "head"), None),
            P("head", "ctx"),
            P("head"),
        ),
        out_specs=(P(("ctx", "head"), None), P(("ctx", "head"), None), P(("ctx", "head"), None)),
        check_vma=False,
    )
```

```python
import jax
import jax.numpy as jnp
from jax import lax
from jax.experimental import pallas as pl
from jax.experimental.pallas import tpu as pltpu
from jax.sharding import PartitionSpec as P


DH = 128
SPAN = 512
HALF = SPAN // 2
SOLVE_STEPS = 8
EPSILON = 1e-06


F32 = jnp.float32
BF16 = jnp.bfloat16


MIB = 1 << 20


def grant(mib, **options):
    return pltpu.CompilerParams(vmem_limit_bytes=mib * MIB, **options)


def in_hbm(array):
    return pltpu.with_memory_space_constraint(array, pltpu.HBM)


def dot(left, right):
    return jnp.dot(left, right, preferred_element_type=F32)


def dot_t(left, right):
    return lax.dot_general(left, right, (((1,), (1,)), ((), ())), preferred_element_type=F32)


def split(value):
    high = value.astype(BF16)
    low = (value - high.astype(F32)).astype(BF16)
    return high, low


def column_of(row):
    return jnp.broadcast_to(row, (DH, row.shape[1])).T


def decay_tile(row, column, start_row, rows, start_col, cols):
    tile = jnp.broadcast_to(row[:, start_col : start_col + cols], (rows, cols))
    wide = jnp.concatenate([column[start_row : start_row + rows]] * (cols // DH), axis=1)
    gap = tile - wide
    if start_row + rows <= start_col:
        return jnp.exp(gap)
    key_pos = start_row + lax.broadcasted_iota(jnp.int32, (rows, cols), 0)
    query_pos = start_col + lax.broadcasted_iota(jnp.int32, (rows, cols), 1)
    return jnp.exp(jnp.where(key_pos <= query_pos, gap, -jnp.inf))


def pack_kernel(a_ref, b_ref, out_ref):
    count = out_ref.shape[0]
    width = a_ref.shape[1] // count
    for j in range(count):
        out_ref[j, :, :width] = a_ref[:, j * width : (j + 1) * width]
        out_ref[j, :, width:] = b_ref[:, j * width : (j + 1) * width]


def pack(a, b, count):
    rows, columns = a.shape
    return pl.pallas_call(
        pack_kernel,
        name="pack",
        out_shape=jax.ShapeDtypeStruct((count, rows, 2 * columns // count), a.dtype),
    )(a, b)


def parts_kernel(own_ref, a_ref, b_ref, *outs):
    width = a_ref.shape[1] // len(outs)
    for d, out_ref in enumerate(outs):
        cols = pl.ds(pl.multiple_of((own_ref[0] ^ d) * width, width), width)
        out_ref[:, :width] = a_ref[:, cols]
        out_ref[:, width:] = b_ref[:, cols]


def column_parts(own, a, b, count):
    rows, columns = a.shape
    return pl.pallas_call(
        parts_kernel,
        name="column_parts",
        compiler_params=grant(4),
        in_specs=[pl.BlockSpec(memory_space=pltpu.SMEM)] + [pl.BlockSpec(memory_space=pltpu.VMEM)] * 2,
        out_shape=[jax.ShapeDtypeStruct((rows, 2 * columns // count), a.dtype)] * count,
    )(own, a, b)


def rows_kernel(own_ref, a_ref, *outs):
    rows = a_ref.shape[0] // len(outs)
    for d, out_ref in enumerate(outs):
        out_ref[...] = a_ref[pl.ds(pl.multiple_of((own_ref[0] ^ d) * rows, rows), rows), :]


def row_parts(own, a, count):
    rows, columns = a.shape
    return pl.pallas_call(
        rows_kernel,
        name="row_parts",
        compiler_params=grant(3),
        in_specs=[pl.BlockSpec(memory_space=pltpu.SMEM), pl.BlockSpec(memory_space=pltpu.VMEM)],
        out_shape=[jax.ShapeDtypeStruct((rows // count, columns), a.dtype)] * count,
    )(own, a)


def trade(parts, axis):
    count = len(parts)
    out = [parts[0]]
    for d in range(1, count):
        out.append(lax.ppermute(parts[d], axis, [(i, i ^ d) for i in range(count)]))
    return out


def unpack_kernel(in_ref, a_ref, b_ref):
    count = in_ref.shape[0]
    width = in_ref.shape[2] // 2
    for j in range(count):
        a_ref[:, j * width : (j + 1) * width] = in_ref[j, :, :width]
        b_ref[:, j * width : (j + 1) * width] = in_ref[j, :, width:]


def unpack(packed):
    count, rows, width = packed.shape
    shape = jax.ShapeDtypeStruct((rows, count * width // 2), packed.dtype)
    return pl.pallas_call(unpack_kernel, name="unpack", compiler_params=grant(4), out_shape=(shape, shape))(packed)


def spread_kernel(own_ref, *refs):
    out_ref = refs[-1]
    for d, in_ref in enumerate(refs[:-1]):
        width = in_ref.shape[1]
        out_ref[:, pl.ds(pl.multiple_of((own_ref[0] ^ d) * width, width), width)] = in_ref[...]


def spread(own, parts):
    rows, width = parts[0].shape
    return pl.pallas_call(
        spread_kernel,
        name="spread",
        compiler_params=grant(3),
        in_specs=[pl.BlockSpec(memory_space=pltpu.SMEM)]
        + [pl.BlockSpec(memory_space=pltpu.VMEM)] * len(parts),
        out_shape=jax.ShapeDtypeStruct((rows, len(parts) * width), parts[0].dtype),
    )(own, *parts)


def gram_kernel(rows_ref, cumul_ref, out_ref, first_ref):
    heads, count = cumul_ref.shape[0], cumul_ref.shape[1]
    pieces = out_ref.shape[0] // heads
    piece = DH // pieces
    for head in range(heads):
        mine = slice(head * DH, (head + 1) * DH)
        other = slice((heads + head) * DH, (heads + head + 1) * DH)
        held = slice(head * pieces, (head + 1) * pieces)
        carry, total = None, 0.0
        for block in range(count):
            rows = slice(block * SPAN, (block + 1) * SPAN)
            keys = rows_ref[rows, mine]
            row = cumul_ref[head, block : block + 1, :]
            last = row[:, SPAN - 1 :]
            weighted = keys.astype(F32).T * jnp.exp(last - row)
            high, low = split(weighted)
            both = jnp.concatenate([keys, rows_ref[rows, other]], axis=1)
            part = dot(high, both) + dot(low, both)
            if block == 0:
                first_ref[head] = part
                carry = part
            else:
                carry = jnp.exp(last) * carry + part
            total = total + last
        out_ref[held, :piece, :] = carry.reshape(pieces, piece, 2 * DH)
        out_ref[held, piece:, :] = jnp.broadcast_to(total[None], (pieces, 8, 2 * DH))


def scan_kernel(in_ref, out_ref, total_ref):
    number, piece = out_ref.shape[0], out_ref.shape[1]
    carry = jnp.zeros(out_ref.shape[1:], F32)
    for j in range(number):
        out_ref[j] = carry
        factor = jnp.exp(in_ref[j, piece:, :])
        total_ref[j] = factor
        carry = factor[:1] * carry + in_ref[j, :piece, :]


def scan_back_kernel(in_ref, total_ref, out_ref):
    carry = jnp.zeros(out_ref.shape[1:], F32)
    for j in reversed(range(out_ref.shape[0])):
        out_ref[j] = carry
        carry = total_ref[j, :1, :] * carry + in_ref[j]


def solve_kernel(
    own_ref,
    rows_ref,
    cumul_ref,
    ridge_ref,
    state_ref,
    first_ref,
    *rest,
):
    parts, rest = rest[:8], rest[8:]
    adjoint_ref, solved_ref, grad_ref, delta_ref, second_ref = rest[:5]
    early, late, stream, keys_t, gathered = rest[5:10]
    weights, solution, residual, direction, images, rhos = zip(rest[10:16], rest[16:])
    head, block = pl.program_id(0), pl.program_id(1)
    count = len(parts)

    @pl.when(jnp.logical_and(head == 0, block == 0))
    def _():
        for d in range(count):
            size = parts[d].shape[0]
            start = pl.multiple_of((own_ref[0] ^ d) * size, size)
            gathered[pl.ds(start, size), :] = parts[d][...]

    rows = pl.ds(pl.multiple_of(block * SPAN, SPAN), SPAN)
    mine = pl.ds(pl.multiple_of(head * DH, DH), DH)
    other = pl.ds(pl.multiple_of((head + 2) * DH, DH), DH)
    keys, values = rows_ref[rows, mine], rows_ref[rows, other]
    row = cumul_ref[head, pl.ds(block, 1), :]
    first_total = cumul_ref[head, 0:1, SPAN - 1 :]
    column = column_of(row)
    start_decay = jnp.exp(row)
    ridge = ridge_ref[head]

    early[...] = decay_tile(row, column, 0, HALF, 0, HALF)
    late[:HALF] = decay_tile(row, column, HALF, HALF, HALF, HALF)
    late[HALF:] = decay_tile(row, column, 0, HALF, HALF, HALF)

    is_late = block == 1
    entry = jnp.where(is_late, jnp.exp(first_total), 1.0)
    local = jnp.where(is_late, 1.0, 0.0)
    state = entry * state_ref[mine] + local * first_ref[head]
    gram_high, gram_low = split(state[:, :DH])
    value_high, value_low = split(state[:, DH:])
    zero = jnp.zeros((HALF, DH), BF16)
    stream[0:HALF] = jnp.concatenate([keys[HALF:], zero], axis=1)
    stream[HALF:SPAN] = jnp.concatenate([keys[:HALF], zero], axis=1)
    stream[SPAN : SPAN + DH] = jnp.concatenate([gram_high, gram_high], axis=1)
    stream[SPAN + DH :] = jnp.concatenate([gram_low, gram_low], axis=1)
    key_t = keys.astype(F32).T.astype(BF16)
    keys_t[:, :HALF] = key_t[:, HALF:]
    keys_t[:, HALF:] = key_t[:, :HALF]

    queries, grads = gathered[rows, mine], gathered[rows, other]
    grad_ref[...] = grads

    query_t = queries.astype(F32).T
    value_rows = jnp.concatenate([value_high, value_low], axis=0)
    for half in range(2):
        cols = slice(half * HALF, (half + 1) * HALF)
        grad_half = grads[cols]
        seen = dot_t(value_rows, grad_half)
        rhs = start_decay[:, cols] * (seen[:DH] + seen[DH:])
        if half == 0:
            masked = (early[...] * dot_t(values[:HALF], grad_half)).astype(BF16)
            rhs = rhs + dot(keys_t[:, HALF:], masked)
        else:
            turned = jnp.concatenate([values[HALF:], values[:HALF]], axis=0)
            masked = (late[...] * dot_t(turned, grad_half)).astype(BF16)
            rhs = rhs + dot(keys_t[...], masked)
        both = jnp.concatenate([query_t[:, cols], rhs], axis=1)
        solution[half][...] = jnp.zeros((DH, SPAN), F32)
        residual[half][...] = both
        direction[half][...] = both
        high, low = split(both)
        weights[half][:DH] = high
        weights[half][DH:] = low

    groups = [slice(g * 16, (g + 1) * 16) for g in range(DH // 16)]

    def column_sum(parts):
        total = parts[0]
        for part in parts[1:]:
            total = total + part
        return jnp.sum(total, axis=0, keepdims=True)

    def norms(half):
        return column_sum([residual[half][g, :] * residual[half][g, :] for g in groups])

    def multiply(half):
        tile, begin = (early, HALF) if half == 0 else (late, 0)
        count = SPAN - begin
        seen = dot(stream[begin:], weights[half][...])
        yield
        scores = []
        for start in range(0, count, 32):
            within = tile[start : start + 32]
            part = seen[start : start + 32]
            scores.append(
                jnp.concatenate(
                    [
                        (within * part[:, :HALF]).astype(BF16),
                        (within * part[:, HALF:]).astype(BF16),
                    ],
                    axis=1,
                )
            )
            yield
        decay = start_decay[:, half * HALF : (half + 1) * HALF]
        decay = jnp.concatenate([decay, decay], axis=1)
        image = dot(keys_t[:, begin:], jnp.concatenate(scores, axis=0))
        for g in groups:
            gram = seen[count + g.start : count + g.stop] + seen[count + DH + g.start : count + DH + g.stop]
            images[half][g, :] = image[g] + decay * gram + ridge * direction[half][g, :]
        yield

    def update(half, last=False):
        rho = rhos[half][...]
        along = 0.0
        for g in groups:
            way = direction[half][g, :]
            along = along + way * images[half][g, :]
            yield
        step = rho / (jnp.sum(along, axis=0, keepdims=True) + EPSILON)
        norm = 0.0
        for g in groups:
            solution[half][g, :] += step * direction[half][g, :]
            if not last:
                left = residual[half][g, :] - step * images[half][g, :]
                residual[half][g, :] = left
                norm = norm + left * left
            yield
        if last:
            return
        rho_next = jnp.sum(norm, axis=0, keepdims=True)
        rhos[half][...] = rho_next
        turn = rho_next / (rho + EPSILON)
        for g in groups:
            way = residual[half][g, :] + turn * direction[half][g, :]
            direction[half][g, :] = way
            high, low = split(way)
            weights[half][g, :] = high
            weights[half][DH + g.start : DH + g.stop, :] = low
            yield

    def weave(multiplying, updating, ratio):
        for _ in multiplying:
            for _ in range(ratio):
                next(updating, None)
        for _ in updating:
            pass

    for half in range(2):
        rhos[half][...] = norms(half)
    for _ in multiply(0):
        pass

    def sweep(_, carry):
        weave(multiply(1), update(0), 1)
        weave(multiply(0), update(1), 2)
        return carry

    lax.fori_loop(0, SOLVE_STEPS - 1, sweep, 0, unroll=True)
    weave(multiply(1), update(0, True), 1)
    for _ in update(1, True):
        pass

    solved_t = jnp.concatenate([solution[0][:, :HALF], solution[1][:, :HALF]], axis=1)
    adjoint_t = jnp.concatenate([solution[0][:, HALF:], solution[1][:, HALF:]], axis=1)
    adjoint = adjoint_t.T.astype(BF16)
    adjoint_ref[...] = adjoint
    solved_ref[...] = solved_t.T.astype(BF16)
    high, low = split(start_decay * solved_t)
    both = jnp.concatenate([grads, -adjoint], axis=1)
    back = dot(high, both) + dot(low, both)

    @pl.when(block == 0)
    def _():
        delta_ref[...] = back

    @pl.when(block == 1)
    def _():
        delta_ref[...] += jnp.exp(first_total) * back
        second_ref[0] = back


def local_kernel(rows_ref, grad_ref, solved_ref, adjoint_ref, cumul_ref, key_out, value_out):
    block = pl.program_id(0)
    heads = cumul_ref.shape[0]
    for head in range(heads):
        here = slice(head * DH, (head + 1) * DH)
        other = slice((heads + head) * DH, (heads + head + 1) * DH)
        keys, values, grads = rows_ref[:, here], rows_ref[:, other], grad_ref[:, here]
        solved, adjoint = solved_ref[:, here], adjoint_ref[:, here]
        row = cumul_ref[head, pl.ds(block, 1), :]
        column = column_of(row)
        left = jnp.concatenate([values, keys], axis=1)
        right = jnp.concatenate([grads, -adjoint], axis=1)
        both = jnp.concatenate([grads, adjoint], axis=1)
        for half in range(2):
            mine = slice(half * HALF, (half + 1) * HALF)
            after = slice(half * HALF, SPAN)
            within = decay_tile(row, column, half * HALF, HALF, half * HALF, SPAN - half * HALF)
            along_solved = (within * dot_t(keys[mine], solved[after])).astype(BF16)
            along = (within * dot_t(left[mine], right[after])).astype(BF16)
            seen = dot(along_solved, both[after])
            value_out[mine, here] = seen[:, :DH]
            key_out[mine, here] = dot(along, solved[after]) - seen[:, DH:]


def final_kernel(rows_ref, state_ref, second_ref, cumul_ref, key_local, value_local, out_ref):
    block = pl.program_id(0)
    heads = cumul_ref.shape[0]
    is_early = block == 0
    local = jnp.where(is_early, 1.0, 0.0)
    for head in range(heads):
        mine = slice(head * DH, (head + 1) * DH)
        other = slice((heads + head) * DH, (heads + head + 1) * DH)
        row = cumul_ref[head, pl.ds(block, 1), :]
        last = cumul_ref[head, 1:2, SPAN - 1 :]
        weight = column_of(jnp.exp(row[:, SPAN - 1 :] - row))
        entry = jnp.where(is_early, jnp.exp(last), 1.0)
        state = entry * state_ref[mine] + local * second_ref[head]
        value_t, gram = state[:, :DH], state[:, DH:]
        upper = jnp.concatenate([value_t, gram + gram.T], axis=1)
        lower = jnp.concatenate([jnp.zeros((DH, DH), F32), value_t.T], axis=1)
        high, low = split(jnp.concatenate([upper, lower], axis=0))
        both = jnp.concatenate([rows_ref[:, mine], rows_ref[:, other]], axis=1)
        seen = dot(both, high) + dot(both, low)
        out_ref[:, mine] = (key_local[:, mine] + weight * seen[:, DH:]).astype(BF16)
        out_ref[:, other] = (value_local[:, mine] + weight * seen[:, :DH]).astype(BF16)


def swap(pieces, axis):
    return lax.all_to_all(pieces, axis, split_axis=0, concat_axis=0, tiled=True)


def shards(queries, keys, values, grads_out, log_decay, ridge):
    heads = lax.axis_size("head")
    number = lax.axis_size("ctx")
    head_dev = log_decay.shape[0]
    tokens = log_decay.shape[1]
    count = tokens // SPAN
    piece = head_dev * DH // number
    grid = (head_dev, count)

    first = swap(pack(keys, values, heads), "head").reshape(tokens, 2 * head_dev * DH)
    own = lax.axis_index("head").astype(jnp.int32).reshape(1)
    parts = trade(column_parts(own, queries, grads_out, heads), "head")
    cumul = jnp.cumsum(log_decay.reshape(head_dev, count, SPAN), axis=2)

    low_spec = pl.BlockSpec((SPAN, DH), lambda h, b: (b, h))
    high_spec = pl.BlockSpec((SPAN, DH), lambda h, b: (b, head_dev + h))
    cumul_spec = pl.BlockSpec((1, count, SPAN), lambda h, b: (h, 0, 0))
    state_spec = pl.BlockSpec((DH, 2 * DH), lambda h, b: (h, 0))
    local_spec = pl.BlockSpec((1, DH, 2 * DH), lambda h, b: (h, 0, 0))
    state_shape = jax.ShapeDtypeStruct((head_dev * DH, 2 * DH), F32)
    local_hbm = pltpu.HBM((head_dev, DH, 2 * DH), F32)

    out, first_state = pl.pallas_call(
        gram_kernel,
        name="gram",
        out_shape=[jax.ShapeDtypeStruct((number, piece + 8, 2 * DH), F32), local_hbm],
        compiler_params=grant(6),
    )(first, cumul)
    prefix, factors = pl.pallas_call(
        scan_kernel,
        name="scan",
        compiler_params=grant(2),
        out_shape=(
            jax.ShapeDtypeStruct((number, piece, 2 * DH), F32),
            jax.ShapeDtypeStruct((number, 8, 2 * DH), F32),
        ),
    )(swap(out, "ctx"))
    state = swap(prefix, "ctx").reshape(head_dev * DH, 2 * DH)

    token_hbm = pltpu.HBM((tokens, head_dev * DH), BF16)
    adjoint, solved, grads_local, delta, second_state = pl.pallas_call(
        solve_kernel,
        name="solve",
        grid=grid,
        in_specs=[
            pl.BlockSpec(memory_space=pltpu.SMEM),
            pl.BlockSpec(memory_space=pltpu.VMEM),
            pl.BlockSpec(memory_space=pltpu.VMEM),
            pl.BlockSpec(memory_space=pltpu.SMEM),
            pl.BlockSpec(memory_space=pltpu.VMEM),
            pl.BlockSpec(memory_space=pltpu.VMEM),
        ]
        + [pl.BlockSpec(memory_space=pltpu.VMEM)] * heads,
        out_specs=[low_spec, low_spec, low_spec, state_spec, local_spec],
        out_shape=[token_hbm, token_hbm, token_hbm, state_shape, local_hbm],
        scratch_shapes=[
            pltpu.VMEM((HALF, HALF), F32),
            pltpu.VMEM((SPAN, HALF), F32),
            pltpu.VMEM((SPAN + 2 * DH, 2 * DH), BF16),
            pltpu.VMEM((DH, SPAN), BF16),
            pltpu.VMEM((tokens, 2 * head_dev * DH), BF16),
        ]
        + [
            pltpu.VMEM((2 * DH, SPAN), BF16),
            pltpu.VMEM((DH, SPAN), F32),
            pltpu.VMEM((DH, SPAN), F32),
            pltpu.VMEM((DH, SPAN), F32),
            pltpu.VMEM((DH, SPAN), F32),
            pltpu.VMEM((1, SPAN), F32),
        ]
        * 2,
        compiler_params=grant(12),
    )(own, first, cumul, in_hbm(ridge), state, first_state, *parts)

    grad_queries = spread(own, trade(row_parts(own, adjoint, heads), "head"))

    def whole(*shape):
        return pl.BlockSpec(shape, lambda b: (0,) * len(shape))

    wide_spec = pl.BlockSpec((SPAN, 2 * head_dev * DH), lambda b: (b, 0))
    narrow_spec = pl.BlockSpec((SPAN, head_dev * DH), lambda b: (b, 0))
    key_local, value_local = pl.pallas_call(
        local_kernel,
        name="local",
        grid=(count,),
        in_specs=[
            wide_spec,
            narrow_spec,
            narrow_spec,
            narrow_spec,
            whole(head_dev, count, SPAN),
        ],
        out_specs=[narrow_spec, narrow_spec],
        out_shape=[pltpu.HBM((tokens, head_dev * DH), F32)] * 2,
        compiler_params=grant(10),
    )(first, grads_local, solved, adjoint, cumul)

    suffix = pl.pallas_call(
        scan_back_kernel,
        name="scan_back",
        compiler_params=grant(2),
        out_shape=jax.ShapeDtypeStruct((number, piece, 2 * DH), F32),
    )(swap(delta.reshape(number, piece, 2 * DH), "ctx"), factors)
    state_after = swap(suffix, "ctx").reshape(head_dev * DH, 2 * DH)

    grads = pl.pallas_call(
        final_kernel,
        name="final",
        grid=(count,),
        in_specs=[
            wide_spec,
            whole(head_dev * DH, 2 * DH),
            whole(head_dev, DH, 2 * DH),
            whole(head_dev, count, SPAN),
            narrow_spec,
            narrow_spec,
        ],
        out_specs=wide_spec,
        out_shape=jax.ShapeDtypeStruct((tokens, 2 * head_dev * DH), BF16),
        compiler_params=grant(10),
    )(first, state_after, second_state, cumul, in_hbm(key_local), in_hbm(value_local))
    grads = swap(grads.reshape(heads, tokens // heads, 2 * head_dev * DH), "head")
    grad_keys, grad_values = unpack(grads)
    return (grad_queries, grad_keys, grad_values)


def solution(mesh):
    return jax.shard_map(
        shards,
        mesh=mesh,
        in_specs=(
            P(("ctx", "head"), None),
            P(("ctx", "head"), None),
            P(("ctx", "head"), None),
            P(("ctx", "head"), None),
            P("head", "ctx"),
            P("head"),
        ),
        out_specs=(P(("ctx", "head"), None), P(("ctx", "head"), None), P(("ctx", "head"), None)),
        check_vma=False,
    )
```

```python
import functools

import jax
import jax.numpy as jnp
from jax import lax
from jax.experimental import pallas as pl
from jax.experimental.pallas import tpu as pltpu
from jax.sharding import PartitionSpec as P


DH = 128
SPAN = 512
HALF = SPAN // 2
SOLVE_STEPS = 8
EPSILON = 1e-06


F32 = jnp.float32
BF16 = jnp.bfloat16


MIB = 1 << 20


def grant(mib, **options):
    return pltpu.CompilerParams(vmem_limit_bytes=mib * MIB, **options)


def in_hbm(array):
    return pltpu.with_memory_space_constraint(array, pltpu.HBM)


def dot(left, right):
    return jnp.dot(left, right, preferred_element_type=F32)


def dot_t(left, right):
    return lax.dot_general(left, right, (((1,), (1,)), ((), ())), preferred_element_type=F32)


def split(value):
    high = value.astype(BF16)
    low = (value - high.astype(F32)).astype(BF16)
    return high, low


def column_of(row):
    return jnp.broadcast_to(row, (DH, row.shape[1])).T


def decay_tile(row, column, start_row, rows, start_col, cols):
    tile = jnp.broadcast_to(row[:, start_col : start_col + cols], (rows, cols))
    wide = jnp.concatenate([column[start_row : start_row + rows]] * (cols // DH), axis=1)
    gap = tile - wide
    if start_row + rows <= start_col:
        return jnp.exp(gap)
    key_pos = start_row + lax.broadcasted_iota(jnp.int32, (rows, cols), 0)
    query_pos = start_col + lax.broadcasted_iota(jnp.int32, (rows, cols), 1)
    return jnp.exp(jnp.where(key_pos <= query_pos, gap, -jnp.inf))


def pack_kernel(a_ref, b_ref, out_ref):
    count = out_ref.shape[0]
    width = a_ref.shape[1] // count
    for j in range(count):
        out_ref[j, :, :width] = a_ref[:, j * width : (j + 1) * width]
        out_ref[j, :, width:] = b_ref[:, j * width : (j + 1) * width]


def pack(a, b, count):
    rows, columns = a.shape
    step = rows // 2
    in_spec = pl.BlockSpec((step, columns), lambda i: (i, 0))
    return pl.pallas_call(
        pack_kernel,
        name="pack",
        grid=(2,),
        in_specs=[in_spec, in_spec],
        out_specs=pl.BlockSpec((count, step, 2 * columns // count), lambda i: (0, i, 0)),
        out_shape=jax.ShapeDtypeStruct((count, rows, 2 * columns // count), a.dtype),
    )(a, b)


def parts_kernel(own_ref, a_ref, b_ref, *outs):
    width = a_ref.shape[1] // len(outs)
    for d, out_ref in enumerate(outs):
        cols = pl.ds(pl.multiple_of((own_ref[0] ^ d) * width, width), width)
        out_ref[:, :width] = a_ref[:, cols]
        out_ref[:, width:] = b_ref[:, cols]


def column_parts(own, a, b, count):
    rows, columns = a.shape
    return pl.pallas_call(
        parts_kernel,
        name="column_parts",
        compiler_params=grant(4),
        in_specs=[pl.BlockSpec(memory_space=pltpu.SMEM)] + [pl.BlockSpec(memory_space=pltpu.VMEM)] * 2,
        out_shape=[jax.ShapeDtypeStruct((rows, 2 * columns // count), a.dtype)] * count,
    )(own, a, b)


def rows_kernel(own_ref, a_ref, *outs):
    rows = a_ref.shape[0] // len(outs)
    for d, out_ref in enumerate(outs):
        out_ref[...] = a_ref[pl.ds(pl.multiple_of((own_ref[0] ^ d) * rows, rows), rows), :]


def row_parts(own, a, count):
    rows, columns = a.shape
    return pl.pallas_call(
        rows_kernel,
        name="row_parts",
        compiler_params=grant(3),
        in_specs=[pl.BlockSpec(memory_space=pltpu.SMEM), pl.BlockSpec(memory_space=pltpu.VMEM)],
        out_shape=[jax.ShapeDtypeStruct((rows // count, columns), a.dtype)] * count,
    )(own, a)


def trade(parts, axis):
    count = len(parts)
    out = [parts[0]]
    for d in range(1, count):
        out.append(lax.ppermute(parts[d], axis, [(i, i ^ d) for i in range(count)]))
    return out


def unpack_kernel(in_ref, a_ref, b_ref):
    count = in_ref.shape[0]
    width = in_ref.shape[2] // 2
    for j in range(count):
        a_ref[:, j * width : (j + 1) * width] = in_ref[j, :, :width]
        b_ref[:, j * width : (j + 1) * width] = in_ref[j, :, width:]


def unpack(packed):
    count, rows, width = packed.shape
    shape = jax.ShapeDtypeStruct((rows, count * width // 2), packed.dtype)
    return pl.pallas_call(unpack_kernel, name="unpack", compiler_params=grant(4), out_shape=(shape, shape))(packed)


def spread_kernel(own_ref, *refs):
    out_ref = refs[-1]
    for d, in_ref in enumerate(refs[:-1]):
        width = in_ref.shape[1]
        out_ref[:, pl.ds(pl.multiple_of((own_ref[0] ^ d) * width, width), width)] = in_ref[...]


def spread(own, parts):
    rows, width = parts[0].shape
    return pl.pallas_call(
        spread_kernel,
        name="spread",
        compiler_params=grant(3),
        in_specs=[pl.BlockSpec(memory_space=pltpu.SMEM)]
        + [pl.BlockSpec(memory_space=pltpu.VMEM)] * len(parts),
        out_shape=jax.ShapeDtypeStruct((rows, len(parts) * width), parts[0].dtype),
    )(own, *parts)


def is_mark(piece, width):
    row = lax.broadcasted_iota(jnp.int32, (DH, width), 0)
    column = lax.broadcasted_iota(jnp.int32, (DH, width), 1)
    return jnp.logical_and(lax.rem(row, piece) == 1, column == 0)


def gram_kernel(rows_ref, cumul_ref, out_ref, first_ref):
    heads, count = cumul_ref.shape[0], cumul_ref.shape[1]
    pieces = out_ref.shape[0] // heads
    piece = DH // pieces
    for head in range(heads):
        mine = slice(head * DH, (head + 1) * DH)
        other = slice((heads + head) * DH, (heads + head + 1) * DH)
        held = slice(head * pieces, (head + 1) * pieces)
        carry, total = None, 0.0
        for block in range(count):
            rows = slice(block * SPAN, (block + 1) * SPAN)
            keys = rows_ref[rows, mine]
            row = cumul_ref[head, block : block + 1, :]
            last = row[:, SPAN - 1 :]
            weighted = keys.astype(F32).T * jnp.exp(last - row)
            high, low = split(weighted)
            both = jnp.concatenate([keys, rows_ref[rows, other]], axis=1)
            part = dot(high, both) + dot(low, both)
            if block == 0:
                first_ref[head] = part
                carry = part
            else:
                carry = jnp.exp(last) * carry + part
            total = total + last
        marked = jnp.where(is_mark(piece, 2 * DH), total, carry)
        out_ref[held] = marked.reshape(pieces, piece, 2 * DH)


def scan_kernel(in_ref, out_ref, total_ref):
    number = out_ref.shape[0]
    carry = jnp.zeros(out_ref.shape[1:], F32)
    for j in range(number):
        out_ref[j] = carry
        part = in_ref[j]
        factor = jnp.exp(part[1:2, 0:1])
        total_ref[j] = jnp.broadcast_to(factor, (8, out_ref.shape[2]))
        carry = factor * carry + part


def scan_back_kernel(in_ref, total_ref, out_ref):
    carry = jnp.zeros(out_ref.shape[1:], F32)
    for j in reversed(range(out_ref.shape[0])):
        out_ref[j] = carry
        carry = total_ref[j, :1, :] * carry + in_ref[j]


def solve_kernel(
    piece,
    own_ref,
    rows_ref,
    cumul_ref,
    ridge_ref,
    state_ref,
    first_ref,
    *rest,
):
    parts, rest = rest[:8], rest[8:]
    adjoint_ref, solved_ref, grad_ref, delta_ref, second_ref = rest[:5]
    early, late, stream, keys_t, gathered = rest[5:10]
    weights, solution, residual, direction, images, rhos = zip(rest[10:16], rest[16:])
    head, block = pl.program_id(0), pl.program_id(1)
    count = len(parts)

    @pl.when(jnp.logical_and(head == 0, block == 0))
    def _():
        for d in range(count):
            size = parts[d].shape[0]
            start = pl.multiple_of((own_ref[0] ^ d) * size, size)
            gathered[pl.ds(start, size), :] = parts[d][...]

    rows = pl.ds(pl.multiple_of(block * SPAN, SPAN), SPAN)
    mine = pl.ds(pl.multiple_of(head * DH, DH), DH)
    other = pl.ds(pl.multiple_of((head + 2) * DH, DH), DH)
    keys, values = rows_ref[rows, mine], rows_ref[rows, other]
    row = cumul_ref[head, pl.ds(block, 1), :]
    first_total = cumul_ref[head, 0:1, SPAN - 1 :]
    column = column_of(row)
    start_decay = jnp.exp(row)
    ridge = ridge_ref[head]

    early[...] = decay_tile(row, column, 0, HALF, 0, HALF)
    late[:HALF] = decay_tile(row, column, HALF, HALF, HALF, HALF)
    late[HALF:] = decay_tile(row, column, 0, HALF, HALF, HALF)

    is_late = block == 1
    entry = jnp.where(is_late, jnp.exp(first_total), 1.0)
    local = jnp.where(is_late, 1.0, 0.0)
    state = state_ref[mine]
    gram = state[:, :DH]
    gram = jnp.where(is_mark(piece, DH), gram.T, gram)
    state = entry * jnp.concatenate([gram, state[:, DH:]], axis=1) + local * first_ref[head]
    gram_high, gram_low = split(state[:, :DH])
    value_high, value_low = split(state[:, DH:])
    zero = jnp.zeros((HALF, DH), BF16)
    stream[0:HALF] = jnp.concatenate([keys[HALF:], zero], axis=1)
    stream[HALF:SPAN] = jnp.concatenate([keys[:HALF], zero], axis=1)
    stream[SPAN : SPAN + DH] = jnp.concatenate([gram_high, gram_high], axis=1)
    stream[SPAN + DH :] = jnp.concatenate([gram_low, gram_low], axis=1)
    key_t = keys.astype(F32).T.astype(BF16)
    keys_t[:, :HALF] = key_t[:, HALF:]
    keys_t[:, HALF:] = key_t[:, :HALF]

    queries, grads = gathered[rows, mine], gathered[rows, other]
    grad_ref[...] = grads

    query_t = queries.astype(F32).T
    value_rows = jnp.concatenate([value_high, value_low], axis=0)
    for half in range(2):
        cols = slice(half * HALF, (half + 1) * HALF)
        grad_half = grads[cols]
        seen = dot_t(value_rows, grad_half)
        rhs = start_decay[:, cols] * (seen[:DH] + seen[DH:])
        if half == 0:
            masked = (early[...] * dot_t(values[:HALF], grad_half)).astype(BF16)
            rhs = rhs + dot(keys_t[:, HALF:], masked)
        else:
            turned = jnp.concatenate([values[HALF:], values[:HALF]], axis=0)
            masked = (late[...] * dot_t(turned, grad_half)).astype(BF16)
            rhs = rhs + dot(keys_t[...], masked)
        both = jnp.concatenate([query_t[:, cols], rhs], axis=1)
        solution[half][...] = jnp.zeros((DH, SPAN), F32)
        residual[half][...] = both
        direction[half][...] = both
        high, low = split(both)
        weights[half][:DH] = high
        weights[half][DH:] = low

    groups = [slice(g * 16, (g + 1) * 16) for g in range(DH // 16)]

    def column_sum(parts):
        total = parts[0]
        for part in parts[1:]:
            total = total + part
        return jnp.sum(total, axis=0, keepdims=True)

    def norms(half):
        return column_sum([residual[half][g, :] * residual[half][g, :] for g in groups])

    def multiply(half):
        tile, begin = (early, HALF) if half == 0 else (late, 0)
        count = SPAN - begin
        seen = dot(stream[begin:], weights[half][...])
        yield
        scores = []
        for start in range(0, count, 32):
            within = tile[start : start + 32]
            part = seen[start : start + 32]
            scores.append(
                jnp.concatenate(
                    [
                        (within * part[:, :HALF]).astype(BF16),
                        (within * part[:, HALF:]).astype(BF16),
                    ],
                    axis=1,
                )
            )
            yield
        decay = start_decay[:, half * HALF : (half + 1) * HALF]
        decay = jnp.concatenate([decay, decay], axis=1)
        image = dot(keys_t[:, begin:], jnp.concatenate(scores, axis=0))
        for g in groups:
            gram = seen[count + g.start : count + g.stop] + seen[count + DH + g.start : count + DH + g.stop]
            images[half][g, :] = image[g] + decay * gram + ridge * direction[half][g, :]
        yield

    def update(half, last=False):
        rho = rhos[half][...]
        along = 0.0
        for g in groups:
            way = direction[half][g, :]
            along = along + way * images[half][g, :]
            yield
        step = rho / (jnp.sum(along, axis=0, keepdims=True) + EPSILON)
        norm = 0.0
        for g in groups:
            solution[half][g, :] += step * direction[half][g, :]
            if not last:
                left = residual[half][g, :] - step * images[half][g, :]
                residual[half][g, :] = left
                norm = norm + left * left
            yield
        if last:
            return
        rho_next = jnp.sum(norm, axis=0, keepdims=True)
        rhos[half][...] = rho_next
        turn = rho_next / (rho + EPSILON)
        for g in groups:
            way = residual[half][g, :] + turn * direction[half][g, :]
            direction[half][g, :] = way
            high, low = split(way)
            weights[half][g, :] = high
            weights[half][DH + g.start : DH + g.stop, :] = low
            yield

    def weave(multiplying, updating, ratio):
        for _ in multiplying:
            for _ in range(ratio):
                next(updating, None)
        for _ in updating:
            pass

    for half in range(2):
        rhos[half][...] = norms(half)
    for _ in multiply(0):
        pass

    def sweep(_, carry):
        weave(multiply(1), update(0), 1)
        weave(multiply(0), update(1), 2)
        return carry

    lax.fori_loop(0, SOLVE_STEPS - 1, sweep, 0, unroll=True)
    weave(multiply(1), update(0, True), 1)
    for _ in update(1, True):
        pass

    solved_t = jnp.concatenate([solution[0][:, :HALF], solution[1][:, :HALF]], axis=1)
    adjoint_t = jnp.concatenate([solution[0][:, HALF:], solution[1][:, HALF:]], axis=1)
    adjoint = adjoint_t.T.astype(BF16)
    adjoint_ref[...] = adjoint
    solved_ref[...] = solved_t.T.astype(BF16)
    high, low = split(start_decay * solved_t)
    both = jnp.concatenate([grads, -adjoint], axis=1)
    back = dot(high, both) + dot(low, both)

    @pl.when(block == 0)
    def _():
        delta_ref[...] = back

    @pl.when(block == 1)
    def _():
        delta_ref[...] += jnp.exp(first_total) * back
        second_ref[0] = back


def local_kernel(rows_ref, grad_ref, solved_ref, adjoint_ref, cumul_ref, key_out, value_out):
    block = pl.program_id(0)
    heads = cumul_ref.shape[0]
    for head in range(heads):
        here = slice(head * DH, (head + 1) * DH)
        other = slice((heads + head) * DH, (heads + head + 1) * DH)
        keys, values, grads = rows_ref[:, here], rows_ref[:, other], grad_ref[:, here]
        solved, adjoint = solved_ref[:, here], adjoint_ref[:, here]
        row = cumul_ref[head, pl.ds(block, 1), :]
        column = column_of(row)
        left = jnp.concatenate([values, keys], axis=1)
        right = jnp.concatenate([grads, -adjoint], axis=1)
        both = jnp.concatenate([grads, adjoint], axis=1)
        for half in range(2):
            mine = slice(half * HALF, (half + 1) * HALF)
            after = slice(half * HALF, SPAN)
            within = decay_tile(row, column, half * HALF, HALF, half * HALF, SPAN - half * HALF)
            along_solved = (within * dot_t(keys[mine], solved[after])).astype(BF16)
            along = (within * dot_t(left[mine], right[after])).astype(BF16)
            seen = dot(along_solved, both[after])
            value_out[mine, here] = seen[:, :DH]
            key_out[mine, here] = dot(along, solved[after]) - seen[:, DH:]


def final_kernel(rows_ref, state_ref, second_ref, cumul_ref, key_local, value_local, out_ref):
    block = pl.program_id(0)
    heads = cumul_ref.shape[0]
    is_early = block == 0
    local = jnp.where(is_early, 1.0, 0.0)
    for head in range(heads):
        mine = slice(head * DH, (head + 1) * DH)
        other = slice((heads + head) * DH, (heads + head + 1) * DH)
        row = cumul_ref[head, pl.ds(block, 1), :]
        last = cumul_ref[head, 1:2, SPAN - 1 :]
        weight = column_of(jnp.exp(row[:, SPAN - 1 :] - row))
        entry = jnp.where(is_early, jnp.exp(last), 1.0)
        state = entry * state_ref[mine] + local * second_ref[head]
        value_t, gram = state[:, :DH], state[:, DH:]
        upper = jnp.concatenate([value_t, gram + gram.T], axis=1)
        lower = jnp.concatenate([jnp.zeros((DH, DH), F32), value_t.T], axis=1)
        high, low = split(jnp.concatenate([upper, lower], axis=0))
        both = jnp.concatenate([rows_ref[:, mine], rows_ref[:, other]], axis=1)
        seen = dot(both, high) + dot(both, low)
        out_ref[:, mine] = (key_local[:, mine] + weight * seen[:, DH:]).astype(BF16)
        out_ref[:, other] = (value_local[:, mine] + weight * seen[:, :DH]).astype(BF16)


def swap(pieces, axis):
    return lax.all_to_all(pieces, axis, split_axis=0, concat_axis=0, tiled=True)


def shards(queries, keys, values, grads_out, log_decay, ridge):
    heads = lax.axis_size("head")
    number = lax.axis_size("ctx")
    head_dev = log_decay.shape[0]
    tokens = log_decay.shape[1]
    count = tokens // SPAN
    piece = head_dev * DH // number
    grid = (head_dev, count)

    first = swap(pack(keys, values, heads), "head").reshape(tokens, 2 * head_dev * DH)
    own = lax.axis_index("head").astype(jnp.int32).reshape(1)
    parts = trade(column_parts(own, queries, grads_out, heads), "head")
    cumul = jnp.cumsum(log_decay.reshape(head_dev, count, SPAN), axis=2)

    low_spec = pl.BlockSpec((SPAN, DH), lambda h, b: (b, h))
    high_spec = pl.BlockSpec((SPAN, DH), lambda h, b: (b, head_dev + h))
    cumul_spec = pl.BlockSpec((1, count, SPAN), lambda h, b: (h, 0, 0))
    state_spec = pl.BlockSpec((DH, 2 * DH), lambda h, b: (h, 0))
    local_spec = pl.BlockSpec((1, DH, 2 * DH), lambda h, b: (h, 0, 0))
    state_shape = jax.ShapeDtypeStruct((head_dev * DH, 2 * DH), F32)
    local_hbm = pltpu.HBM((head_dev, DH, 2 * DH), F32)

    out, first_state = pl.pallas_call(
        gram_kernel,
        name="gram",
        out_shape=[jax.ShapeDtypeStruct((number, piece, 2 * DH), F32), local_hbm],
        compiler_params=grant(6),
    )(first, cumul)
    prefix, factors = pl.pallas_call(
        scan_kernel,
        name="scan",
        compiler_params=grant(2),
        out_shape=(
            jax.ShapeDtypeStruct((number, piece, 2 * DH), F32),
            jax.ShapeDtypeStruct((number, 8, 2 * DH), F32),
        ),
    )(swap(out, "ctx"))
    state = swap(prefix, "ctx").reshape(head_dev * DH, 2 * DH)

    token_hbm = pltpu.HBM((tokens, head_dev * DH), BF16)
    adjoint, solved, grads_local, delta, second_state = pl.pallas_call(
        functools.partial(solve_kernel, piece),
        name="solve",
        grid=grid,
        in_specs=[
            pl.BlockSpec(memory_space=pltpu.SMEM),
            pl.BlockSpec(memory_space=pltpu.VMEM),
            pl.BlockSpec(memory_space=pltpu.VMEM),
            pl.BlockSpec(memory_space=pltpu.SMEM),
            pl.BlockSpec(memory_space=pltpu.VMEM),
            pl.BlockSpec(memory_space=pltpu.VMEM),
        ]
        + [pl.BlockSpec(memory_space=pltpu.VMEM)] * heads,
        out_specs=[low_spec, low_spec, low_spec, state_spec, local_spec],
        out_shape=[token_hbm, token_hbm, token_hbm, state_shape, local_hbm],
        scratch_shapes=[
            pltpu.VMEM((HALF, HALF), F32),
            pltpu.VMEM((SPAN, HALF), F32),
            pltpu.VMEM((SPAN + 2 * DH, 2 * DH), BF16),
            pltpu.VMEM((DH, SPAN), BF16),
            pltpu.VMEM((tokens, 2 * head_dev * DH), BF16),
        ]
        + [
            pltpu.VMEM((2 * DH, SPAN), BF16),
            pltpu.VMEM((DH, SPAN), F32),
            pltpu.VMEM((DH, SPAN), F32),
            pltpu.VMEM((DH, SPAN), F32),
            pltpu.VMEM((DH, SPAN), F32),
            pltpu.VMEM((1, SPAN), F32),
        ]
        * 2,
        compiler_params=grant(12),
    )(own, first, cumul, in_hbm(ridge), state, first_state, *parts)

    grad_queries = spread(own, trade(row_parts(own, adjoint, heads), "head"))

    def whole(*shape):
        return pl.BlockSpec(shape, lambda b: (0,) * len(shape))

    wide_spec = pl.BlockSpec((SPAN, 2 * head_dev * DH), lambda b: (b, 0))
    narrow_spec = pl.BlockSpec((SPAN, head_dev * DH), lambda b: (b, 0))
    key_local, value_local = pl.pallas_call(
        local_kernel,
        name="local",
        grid=(count,),
        in_specs=[
            wide_spec,
            narrow_spec,
            narrow_spec,
            narrow_spec,
            whole(head_dev, count, SPAN),
        ],
        out_specs=[narrow_spec, narrow_spec],
        out_shape=[pltpu.HBM((tokens, head_dev * DH), F32)] * 2,
        compiler_params=grant(10),
    )(first, grads_local, solved, adjoint, cumul)

    suffix = pl.pallas_call(
        scan_back_kernel,
        name="scan_back",
        compiler_params=grant(2),
        out_shape=jax.ShapeDtypeStruct((number, piece, 2 * DH), F32),
    )(swap(delta.reshape(number, piece, 2 * DH), "ctx"), factors)
    state_after = swap(suffix, "ctx").reshape(head_dev * DH, 2 * DH)

    grads = pl.pallas_call(
        final_kernel,
        name="final",
        grid=(count,),
        in_specs=[
            wide_spec,
            whole(head_dev * DH, 2 * DH),
            whole(head_dev, DH, 2 * DH),
            whole(head_dev, count, SPAN),
            narrow_spec,
            narrow_spec,
        ],
        out_specs=wide_spec,
        out_shape=jax.ShapeDtypeStruct((tokens, 2 * head_dev * DH), BF16),
        compiler_params=grant(10),
    )(first, state_after, second_state, cumul, in_hbm(key_local), in_hbm(value_local))
    grads = swap(grads.reshape(heads, tokens // heads, 2 * head_dev * DH), "head")
    grad_keys, grad_values = unpack(grads)
    return (grad_queries, grad_keys, grad_values)


def solution(mesh):
    return jax.shard_map(
        shards,
        mesh=mesh,
        in_specs=(
            P(("ctx", "head"), None),
            P(("ctx", "head"), None),
            P(("ctx", "head"), None),
            P(("ctx", "head"), None),
            P("head", "ctx"),
            P("head"),
        ),
        out_specs=(P(("ctx", "head"), None), P(("ctx", "head"), None), P(("ctx", "head"), None)),
        check_vma=False,
    )
```
